32 devices in a mesh: dp: 4 (over y, core), mp: 8 (over z, x).
Axes of the slice: x: 2, y: 2, z: 4, core: 2. Of those that a mesh axis runs over, the one named last changes fastest.
Arguments:
- features: bfloat16 [1024, 4, 576], P('mp', 'dp'), may hold values from -6 to 6
- position: bfloat16 [1024, 576], P('mp'), may hold values from -3 to 3
- image_sizes: int32 [4], P('dp'), may hold values from 16 to 24, as said below
- gain_early: float32 [1024], P('mp'), may hold values from 0.5 to 1.5
- bias_early: float32 [1024], P('mp'), may hold values from -2 to 2
- conv_early: bfloat16 [1024, 9, 1024], P(None, None, 'mp'), may hold values from -0.0625 to 0.0625
- conv_bias_early: float32 [1024], P('mp'), may hold values from -4 to 4
- squeeze_down_early: float32 [1024, 256], P('mp'), may hold values from -0.1875 to 0.1875
- squeeze_down_bias_early: float32 [256], replicated, may hold values from -3 to 3
- squeeze_up_early: float32 [256, 1024], P(None, 'mp'), may hold values from -0.375 to 0.375
- squeeze_up_bias_early: float32 [1024], P('mp'), may hold values from -3 to 3
- gain_late: float32 [1024], P('mp'), may hold values from 0.5 to 1.5
- bias_late: float32 [1024], P('mp'), may hold values from -2 to 2
- conv_late: bfloat16 [1024, 9, 1024], P(None, None, 'mp'), may hold values from -0.0625 to 0.0625
- conv_bias_late: float32 [1024], P('mp'), may hold values from -4 to 4
- squeeze_down_late: float32 [1024, 256], P('mp'), may hold values from -0.1875 to 0.1875
- squeeze_down_bias_late: float32 [256], replicated, may hold values from -3 to 3
- squeeze_up_late: float32 [256, 1024], P(None, 'mp'), may hold values from -0.375 to 0.375
- squeeze_up_bias_late: float32 [1024], P('mp'), may hold values from -3 to 3
- readout_in: bfloat16 [1024, 4096], P(None, 'mp'), may hold values from -0.1875 to 0.1875
- readout_in_bias: float32 [4096], P('mp'), may hold values from -3 to 3
- readout_out: bfloat16 [4096, 4096], P(None, 'mp'), may hold values from -0.09375 to 0.09375
- readout_out_bias: float32 [4096], P('mp'), may hold values from -3 to 3
- out_grad: bfloat16 [576, 4096], P('dp', 'mp'), may hold values from -6 to 6
Outputs:
- tokens_out: bfloat16 [576, 4096], P('dp', 'mp')
- features_grad: float32 [1024, 4, 576], P('mp', 'dp')
- position_grad: float32 [1024, 576], P('mp')
- grad_gain_early: float32 [1024], P('mp')
- grad_bias_early: float32 [1024], P('mp')
- grad_conv_early: float32 [1024, 9, 1024], P(None, None, 'mp')
- grad_conv_bias_early: float32 [1024], P('mp')
- grad_down_early: float32 [1024, 256], P('mp')
- grad_down_bias_early: float32 [256], replicated
- grad_up_early: float32 [256, 1024], P(None, 'mp')
- grad_up_bias_early: float32 [1024], P('mp')
- grad_gain_late: float32 [1024], P('mp')
- grad_bias_late: float32 [1024], P('mp')
- grad_conv_late: float32 [1024, 9, 1024], P(None, None, 'mp')
- grad_conv_bias_late: float32 [1024], P('mp')
- grad_down_late: float32 [1024, 256], P('mp')
- grad_down_bias_late: float32 [256], replicated
- grad_up_late: float32 [256, 1024], P(None, 'mp')
- grad_up_bias_late: float32 [1024], P('mp')
- grad_readout_in: float32 [1024, 4096], P(None, 'mp')
- grad_readout_in_bias: float32 [4096], P('mp')
- grad_readout_out: float32 [4096, 4096], P(None, 'mp')
- grad_readout_out_bias: float32 [4096], P('mp')
The draws below stay inside these ranges and needn't reach their ends.
Inputs may be any that keep to these rules, and one draw needn't show every extreme that they name: `image_sizes`: each entry is 16 or 24, and both occur.
All inputs are finite; a program needn't handle non-finite values.
Results may differ from the reference program's by a relative error of at most 0.0064.
Values may be sent and summed in bfloat16 or wider, within the bound.
No kernel may reach another device: no remote copies, remote signals or barrier semaphores. Data moves between devices by JAX's collectives and lax.ppermute only.
A program may use at most 128 MiB of HBM per device.

```python
from functools import partial
import jax
import jax.numpy as jnp
from jax import lax

D = 1024
HID = 4096
SE = 256
SIDE = 24
SMALL = 16
GRID = 12
IMAGES = 4


def draw_image_sizes(key, part):
    picks = jax.random.randint(key, (IMAGES,), 0, 2)
    sizes_drawn = jnp.where(picks == 1, SIDE, SMALL).astype(jnp.int32)
    return sizes_drawn.at[0].set(SIDE).at[1].set(SMALL)


def block_scale(stream_key, dims, split, smallest, high):
    factor_of = 1.0
    for dim, shards_of in split:
        draws = jax.random.uniform(jax.random.fold_in(jax.random.fold_in(stream_key, 6), dim), (shards_of,), jnp.float32, smallest / len(split), high / len(split))
        factor_of = factor_of * jnp.repeat(jnp.exp(draws), dims[dim] // shards_of).reshape((-1,) + (1,) * (len(dims) - 1 - dim))
    return factor_of


def gaussian(own_key, shape, scale, reach, shards=(), dtype=jnp.bfloat16):
    values = scale * jax.random.normal(own_key, shape, jnp.float32)
    if shards:
        values = values * block_scale(own_key, shape, shards, -0.22, 0.18)
    return jnp.clip(values, -reach, reach).astype(dtype)


def setup_inputs(seed: int = 0) -> dict:
    key_list = jax.random.split(jax.random.key(seed), 25)
    return {
        "features": gaussian(key_list[0], (D, IMAGES, SIDE * SIDE), 1.0, 6.0, ((0, 8), (1, 4))),
        "position": gaussian(key_list[1], (D, SIDE * SIDE), 0.5, 3.0, ((0, 8),)),
        "image_sizes": draw_image_sizes(jax.random.fold_in(key_list[24], 71), 0),
        "gain_early": jnp.clip(1.0 + 0.1 * jax.random.normal(key_list[3], (D,), jnp.float32), 0.5, 1.5),
        "bias_early": gaussian(key_list[4], (D,), 0.3, 2.0, ((0, 8),), jnp.float32),
        "conv_early": gaussian(key_list[5], (D, 9, D), (9 * D) ** -0.5, 0.0625, ((2, 8),)),
        "conv_bias_early": gaussian(key_list[6], (D,), 1.0, 4.0, ((0, 8),), jnp.float32),
        "squeeze_down_early": gaussian(key_list[7], (D, SE), D ** -0.5, 0.1875, ((0, 8),), jnp.float32),
        "squeeze_down_bias_early": gaussian(key_list[8], (SE,), 0.5, 3.0, (), jnp.float32),
        "squeeze_up_early": gaussian(key_list[9], (SE, D), SE ** -0.5, 0.375, ((1, 8),), jnp.float32),
        "squeeze_up_bias_early": gaussian(key_list[10], (D,), 0.5, 3.0, ((0, 8),), jnp.float32),
        "gain_late": jnp.clip(1.0 + 0.1 * jax.random.normal(key_list[11], (D,), jnp.float32), 0.5, 1.5),
        "bias_late": gaussian(key_list[12], (D,), 0.3, 2.0, ((0, 8),), jnp.float32),
        "conv_late": gaussian(key_list[13], (D, 9, D), (9 * D) ** -0.5, 0.0625, ((2, 8),)),
        "conv_bias_late": gaussian(key_list[14], (D,), 1.0, 4.0, ((0, 8),), jnp.float32),
        "squeeze_down_late": gaussian(key_list[15], (D, SE), D ** -0.5, 0.1875, ((0, 8),), jnp.float32),
        "squeeze_down_bias_late": gaussian(key_list[16], (SE,), 0.5, 3.0, (), jnp.float32),
        "squeeze_up_late": gaussian(key_list[17], (SE, D), SE ** -0.5, 0.375, ((1, 8),), jnp.float32),
        "squeeze_up_bias_late": gaussian(key_list[18], (D,), 0.5, 3.0, ((0, 8),), jnp.float32),
        "readout_in": gaussian(key_list[19], (D, HID), D ** -0.5, 0.1875, ((1, 8),)),
        "readout_in_bias": gaussian(key_list[20], (HID,), 0.5, 3.0, ((0, 8),), jnp.float32),
        "readout_out": gaussian(key_list[21], (HID, HID), HID ** -0.5, 0.09375, ((1, 8),)),
        "readout_out_bias": gaussian(key_list[22], (HID,), 0.5, 3.0, ((0, 8),), jnp.float32),
        "out_grad": gaussian(key_list[23], (IMAGES * GRID * GRID, HID), 1.0, 6.0, ((0, 4), (1, 8))),
    }


@jax.custom_vjp
def low(v):
    return lax.optimization_barrier(v.astype(jnp.bfloat16)).astype(jnp.float32)

@jax.custom_vjp
def low_back(v):
    return v

def low_keep(v):
    return (low(v), None)

def low_pass(kept, grad):
    return (grad,)

def back_keep(v):
    return (v, None)

def back_low(kept, grad):
    return (low(grad),)
low.defvjp(low_keep, low_pass)
low_back.defvjp(back_keep, back_low)
highest_precision = lax.Precision.HIGHEST
epsilon = 1e-06

def pool_matrix(extent, side_len, grid_len):
    row_index = jnp.arange(grid_len)[:, None]
    col_index = jnp.arange(side_len)[None, :]
    first_col = row_index * extent // grid_len
    end_col = -(-(row_index + 1) * extent // grid_len)
    in_bin = (col_index >= first_col) & (col_index < end_col)
    return jnp.where(in_bin, 1.0, 0.0).astype(jnp.float32) / (end_col - first_col).astype(jnp.float32)

def convolve(inputs, kernel):
    kernel_grid = jnp.transpose(kernel, (1, 0, 2)).reshape(3, 3, kernel.shape[0], kernel.shape[2])
    return lax.conv_general_dilated(inputs, kernel_grid, (1, 1), 'SAME', dimension_numbers=('NHWC', 'HWIO', 'NHWC'), precision=highest_precision)

def squeeze_block(inputs, valid_mask, counts, norm_gain, norm_bias, kernel, conv_bias, se_down, se_down_bias, se_up, se_up_bias):
    center = lax.optimization_barrier(jnp.mean(inputs, axis=-1, keepdims=True))
    spread = lax.optimization_barrier(jnp.mean(jnp.square(inputs - center), axis=-1, keepdims=True))
    normed = (inputs - center) * lax.rsqrt(spread + epsilon)
    hidden = low(jax.nn.silu(normed * norm_gain + norm_bias) * valid_mask)
    conv_out = low_back(convolve(hidden, kernel) + conv_bias) * valid_mask
    squeezed = lax.optimization_barrier(jnp.sum(conv_out, axis=(1, 2))) / counts[:, None]
    reduced = jax.nn.silu(jnp.dot(squeezed, se_down, precision=highest_precision) + se_down_bias)
    excite = jax.nn.sigmoid(jnp.dot(reduced, se_up, precision=highest_precision) + se_up_bias)
    return inputs + conv_out * excite[:, None, None, :]

def forward(image_sizes, features, position, *weights):
    early = weights[0:8]
    late = weights[8:16]
    readout_in, readout_in_bias, readout_out, readout_out_bias = weights[16:20]
    channels = features.shape[0]
    images = features.shape[1]
    grid_in = jnp.transpose(features.reshape(channels, images, SIDE, SIDE), (1, 2, 3, 0))
    pos_grid = jnp.transpose(position.reshape(channels, SIDE, SIDE), (1, 2, 0))
    extent = jnp.arange(SIDE)
    in_rows = extent[None, :] < image_sizes[:, None]
    valid_mask = jnp.where(in_rows[:, :, None] & in_rows[:, None, :], 1.0, 0.0).astype(jnp.float32)[..., None]
    counts = (image_sizes * image_sizes).astype(jnp.float32)
    start_grid = (grid_in + pos_grid) * valid_mask
    early_block_output = squeeze_block(start_grid, valid_mask, counts, *early)
    lookup_tables = jnp.where((image_sizes == SIDE)[:, None, None], pool_matrix(SIDE, SIDE, GRID)[None], pool_matrix(SMALL, SIDE, GRID)[None])
    pooled_tokens = jnp.einsum('tpo,tonh->tpnh', lookup_tables, early_block_output, precision=highest_precision)
    pooled_tokens = jnp.einsum('ibc,iacd->iabd', lookup_tables, pooled_tokens, precision=highest_precision)
    full_mask = jnp.ones((images, GRID, GRID, 1), jnp.float32)
    grid_counts = jnp.full((images,), GRID * GRID, jnp.float32)
    after_late = squeeze_block(pooled_tokens, full_mask, grid_counts, *late)
    tokens = low(after_late.reshape(images * GRID * GRID, channels))
    pre_gelu = low_back(jnp.dot(tokens, readout_in, precision=highest_precision) + readout_in_bias)
    hidden_act = low(jax.nn.gelu(pre_gelu, approximate=False))
    return jnp.dot(hidden_act, readout_out, precision=highest_precision) + readout_out_bias

def reference(features, position, image_sizes, gain_early, bias_early, conv_early, conv_bias_early, squeeze_down_early, squeeze_down_bias_early, squeeze_up_early, squeeze_up_bias_early, gain_late, bias_late, conv_late, conv_bias_late, squeeze_down_late, squeeze_down_bias_late, squeeze_up_late, squeeze_up_bias_late, readout_in, readout_in_bias, readout_out, readout_out_bias, out_grad):
    inputs_all = (features, position, gain_early, bias_early, conv_early, conv_bias_early, squeeze_down_early, squeeze_down_bias_early, squeeze_up_early, squeeze_up_bias_early, gain_late, bias_late, conv_late, conv_bias_late, squeeze_down_late, squeeze_down_bias_late, squeeze_up_late, squeeze_up_bias_late, readout_in, readout_in_bias, readout_out, readout_out_bias)
    floats = tuple((entry.astype(jnp.float32) for entry in inputs_all))
    forward_all = partial(forward, image_sizes)
    result, pullback = jax.vjp(forward_all, *floats)
    gradients = pullback(out_grad.astype(jnp.float32))
    return (result.astype(jnp.bfloat16), gradients[0], gradients[1], gradients[2], gradients[3], gradients[4], gradients[5], gradients[6], gradients[7], gradients[8], gradients[9], gradients[10], gradients[11], gradients[12], gradients[13], gradients[14], gradients[15], gradients[16], gradients[17], gradients[18], gradients[19], gradients[20], gradients[21])
```

```python
from functools import partial

import jax
import jax.numpy as jnp
from jax import lax
from jax.experimental import pallas as pl
from jax.experimental.pallas import tpu as pltpu
from jax.sharding import PartitionSpec as P

SIDE = 24
SMALL = 16
GRID = 12
EPS = 1e-06
F32 = jnp.float32
BF16 = jnp.bfloat16
HI = lax.Precision.HIGHEST


def pool_matrix(extent, side_len, grid_len):
    row_index = jnp.arange(grid_len)[:, None]
    col_index = jnp.arange(side_len)[None, :]
    first_col = row_index * extent // grid_len
    end_col = -(-(row_index + 1) * extent // grid_len)
    in_bin = (col_index >= first_col) & (col_index < end_col)
    return jnp.where(in_bin, 1.0, 0.0).astype(F32) / (end_col - first_col).astype(F32)


def shape(dims, dtype=F32):
    return jax.ShapeDtypeStruct(dims, dtype)


def cost(flops, nbytes):
    return pl.CostEstimate(flops=int(flops), bytes_accessed=int(nbytes), transcendentals=0)


def call(kernel, outs, *args, flops=1e6, smem=(), name=None):
    specs = [
        pl.BlockSpec(memory_space=pltpu.SMEM if k in smem else pltpu.VMEM)
        for k in range(len(args))
    ]
    nbytes = sum(a.size * a.dtype.itemsize for a in args) + sum(
        o.size * jnp.dtype(o.dtype).itemsize for o in outs
    )
    return pl.pallas_call(
        kernel,
        out_shape=list(outs),
        in_specs=specs,
        out_specs=[pl.BlockSpec(memory_space=pltpu.VMEM) for _ in outs],
        cost_estimate=cost(flops, nbytes),
        name=name,
    )(*args)


def mm(a, b, ca, cb, precision=None):
    return lax.dot_general(
        a, b, (((ca,), (cb,)), ((), ())), preferred_element_type=F32, precision=precision
    )


def sigmoid(v):
    return 1.0 / (1.0 + jnp.exp(-v))


def silu_grad(v):
    s = sigmoid(v)
    return s * (1.0 + v * (1.0 - s))


def grid_rc(side, lanes):
    i = lax.broadcasted_iota(jnp.int32, (side * side, lanes), 0).astype(F32)
    r = jnp.floor((i + 0.5) * (1.0 / side))
    return r, i - r * side


def tap_ok(r, c, side, dy, dx):
    ok = None
    for v, d in ((r, dy), (c, dx)):
        if d == 0:
            continue
        one = (v >= 0.5) if d < 0 else (v <= side - 1.5)
        ok = one if ok is None else ok & one
    return ok


def tap_sum(y, side, width):
    n = side * side
    r, c = grid_rc(side, width)
    total = None
    for t in range(9):
        dy, dx = t // 3 - 1, t % 3 - 1
        part = y[:, t * width : (t + 1) * width]
        off = dy * side + dx
        if off:
            part = pltpu.roll(part, (-off) % n, 0)
        ok = tap_ok(r, c, side, dy, dx)
        if ok is not None:
            part = jnp.where(ok, part, 0.0)
        total = part if total is None else total + part
    return total


def tap_spread(g, side, width):
    n = side * side
    r, c = grid_rc(side, width)
    parts = []
    for t in range(9):
        dy, dx = t // 3 - 1, t % 3 - 1
        off = dy * side + dx
        part = pltpu.roll(g, off % n, 0) if off else g
        ok = tap_ok(r, c, side, -dy, -dx)
        if ok is not None:
            part = jnp.where(ok, part, 0.0)
        parts.append(part.astype(BF16))
    return jnp.concatenate(parts, axis=1)


def wide(ref):
    return jnp.concatenate([ref[j] for j in range(ref.shape[0])], axis=1)


def split_mm(p, v, ca, cb):
    top = v.astype(BF16)
    low = (v - top.astype(F32)).astype(BF16)
    return mm(p, top, ca, cb) + mm(p, low, ca, cb)


def size_mask(size, width):
    r, c = grid_rc(SIDE, width)
    s = size.astype(F32) - 0.5
    return jnp.where((r < s) & (c < s), 1.0, 0.0).astype(F32)


def put_all(ref, value):
    for j in range(ref.shape[0]):
        ref[j] = value


def rows_of(pair_ref, total):
    acc = pair_ref[0]
    for j in range(1, total):
        acc = acc + pair_ref[j]
    return acc


def row_sums(u, v):
    ones = jnp.ones((8, u.shape[1]), F32)
    su = mm(ones, u, 1, 1, HI)
    sv = mm(ones, v, 1, 1, HI)
    row = lax.broadcasted_iota(jnp.int32, su.shape, 0)
    return jnp.where(row < 4, su, sv)


def spread_rows(acc, which, width):
    row = lax.broadcasted_iota(jnp.int32, (8, width), 0)
    pick = jnp.where(row == which, 1.0, 0.0).astype(F32)
    return mm(acc, pick, 0, 0, HI)


def prep_kernel(size_ref, f_ref, p_ref, x_ref, s_ref):
    width = f_ref.shape[1]
    x = (f_ref[...].astype(F32) + p_ref[...].astype(F32)) * size_mask(size_ref[0], width)
    x_ref[...] = x
    put_all(s_ref, row_sums(x, x * x))


def hidden_kernel(channels, size_ref, x_ref, s_ref, gain_ref, bias_ref, out_ref, mom_ref):
    width = x_ref.shape[1]
    acc = rows_of(s_ref, s_ref.shape[0]) * (1.0 / channels)
    center = spread_rows(acc, 0, width)
    square = spread_rows(acc, 4, width)
    inv = lax.rsqrt(square - center * center + EPS)
    mom_ref[0] = center
    mom_ref[1] = inv
    pre = (x_ref[...] - center) * inv * gain_ref[...] + bias_ref[...]
    hid = (pre * sigmoid(pre) * size_mask(size_ref[0], width)).astype(BF16)
    put_all(out_ref, hid)


def conv_kernel(
    size_ref, h_ref, w_ref, cb_ref, x_ref, pp_ref, down_ref, conv_ref, a_ref, b_ref, sq_ref, rp_ref
):
    out = w_ref.shape[2]
    h = wide(h_ref)
    y = mm(h, wide(w_ref), 1, 0)
    size = size_ref[0].astype(F32)
    conv = (tap_sum(y, SIDE, out) + cb_ref[...]) * size_mask(size_ref[0], out)
    conv_ref[...] = conv
    a_ref[...] = split_mm(pp_ref[...], x_ref[...], 1, 0)
    b_ref[...] = split_mm(pp_ref[...], conv, 1, 0)
    sq = jnp.sum(conv, axis=0, keepdims=True) * (1.0 / (size * size + jnp.zeros((1, out), F32)))
    sq_ref[...] = sq
    put_all(rp_ref, mm(jnp.broadcast_to(sq, (8, out)), down_ref[...], 1, 0, HI))


def excite_of(rp_ref, db_ref, up_ref, ub_ref):
    rpre = rows_of(rp_ref, rp_ref.shape[0]) + db_ref[...]
    red = rpre * sigmoid(rpre)
    e = sigmoid(mm(red, up_ref[...], 1, 0, HI) + ub_ref[...])
    return rpre[0:1], e[0:1]


def pooled_kernel(rp_ref, db_ref, up_ref, ub_ref, a_ref, b_ref, out_ref, rpre_ref, e_ref):
    rpre, e = excite_of(rp_ref, db_ref, up_ref, ub_ref)
    rpre_ref[...] = rpre
    e_ref[...] = e
    put_all(out_ref, (a_ref[...] + b_ref[...] * e).astype(out_ref.dtype))


def late_norm(pool_ref, gain_ref, bias_ref):
    x = wide(pool_ref).astype(F32)
    channels = x.shape[1]
    center = jnp.sum(x, axis=1, keepdims=True) * (1.0 / channels)
    d = x - center
    inv = lax.rsqrt(jnp.sum(d * d, axis=1, keepdims=True) * (1.0 / channels) + EPS)
    normed = d * inv
    return normed, inv, normed * gain_ref[...] + bias_ref[...]


def late_kernel(
    pool_ref, gain_ref, bias_ref, w_ref, cb_ref, down_ref, h_ref, conv_ref, sq_ref, rp_ref
):
    out = w_ref.shape[2]
    _, _, pre = late_norm(pool_ref, gain_ref, bias_ref)
    h = (pre * sigmoid(pre)).astype(BF16)
    h_ref[...] = h
    y = mm(h, wide(w_ref), 1, 0)
    conv = tap_sum(y, GRID, out) + cb_ref[...]
    conv_ref[...] = conv
    sq = jnp.sum(conv, axis=0, keepdims=True) * (1.0 / (GRID * GRID))
    sq_ref[...] = sq
    put_all(rp_ref, mm(jnp.broadcast_to(sq, (8, out)), down_ref[...], 1, 0, HI))


def late_slope_kernel(pool_ref, gain_ref, bias_ref, n_ref, i_ref, d_ref):
    normed, inv, pre = late_norm(pool_ref, gain_ref, bias_ref)
    n_ref[...] = normed
    i_ref[...] = jnp.broadcast_to(inv, i_ref.shape)
    d_ref[...] = silu_grad(pre)


def token_kernel(rp_ref, db_ref, up_ref, ub_ref, pool_ref, conv_ref, out_ref, rpre_ref, e_ref):
    rpre, e = excite_of(rp_ref, db_ref, up_ref, ub_ref)
    rpre_ref[...] = rpre
    e_ref[...] = e
    put_all(out_ref, (pool_ref[...] + conv_ref[...] * e).astype(BF16))


def readout_kernel(t_ref, w_ref, b_ref, gh_ref, act_ref, gp_ref, gt_ref):
    pre = mm(wide(t_ref), w_ref[...], 1, 0) + b_ref[...]
    phi = 0.5 * (1.0 + lax.erf(pre * 0.7071067811865476))
    act_ref[...] = (pre * phi).astype(BF16)
    dens = 0.3989422804014327 * jnp.exp(-0.5 * pre * pre)
    gh = gh_ref[0].astype(F32)
    for j in range(1, gh_ref.shape[0]):
        gh = gh + gh_ref[j].astype(F32)
    gp = (gh * (phi + pre * dens)).astype(BF16)
    gp_ref[...] = gp
    gt = mm(gp, w_ref[...], 1, 1)
    step = gt_ref.shape[2]
    for j in range(gt_ref.shape[0]):
        gt_ref[j] = gt[:, j * step : (j + 1) * step].astype(BF16)


def act_grad_kernel(g_ref, w_ref, out_ref):
    out_ref[0] = mm(g_ref[...], w_ref[...], 1, 1).astype(BF16)


def logits_kernel(act_ref, w_ref, b_ref, out_ref, acc_ref):
    j = pl.program_id(0)
    part = mm(act_ref[0], w_ref[...], 1, 0)

    @pl.when(j == 0)
    def _():
        acc_ref[...] = part

    @pl.when(j > 0)
    def _():
        acc_ref[...] += part

    @pl.when(j == pl.num_programs(0) - 1)
    def _():
        out_ref[...] = (acc_ref[...] + b_ref[...]).astype(BF16)


def excite_back(g, conv, e_ref, up_ref, gl_ref):
    e = e_ref[...]
    gl = jnp.sum(g * conv, axis=0, keepdims=True) * e * (1.0 - e)
    gl_ref[...] = gl
    return mm(jnp.broadcast_to(gl, (8, gl.shape[1])), up_ref[...], 1, 1, HI)


def late_back_a(gt_ref, conv_ref, e_ref, up_ref, g_ref, gl_ref, gr_ref):
    g = gt_ref[0].astype(F32)
    for j in range(1, gt_ref.shape[0]):
        g = g + gt_ref[j].astype(F32)
    g_ref[...] = g
    put_all(gr_ref, excite_back(g, conv_ref[...], e_ref, up_ref, gl_ref))


def squeeze_back(gr, rpre_ref, down_ref, grp_ref):
    rp = rpre_ref[...]
    grp = gr * silu_grad(rp)
    grp_ref[...] = grp[0:1]
    return mm(grp, down_ref[...], 1, 1, HI)[0:1]


def late_back_b(
    gr_ref, rpre_ref, down_ref, e_ref, g_ref, w_ref, n_ref, i_ref, d_ref, gain_ref,
    gc_ref, grp_ref, part_ref, gg_ref,
):
    out = w_ref.shape[2]
    gs = squeeze_back(rows_of(gr_ref, gr_ref.shape[0]), rpre_ref, down_ref, grp_ref)
    gc = (g_ref[...] * e_ref[...] + gs * (1.0 / (GRID * GRID))).astype(BF16)
    gc_ref[...] = gc
    spread = tap_spread(gc.astype(F32), GRID, out)
    gh = mm(spread, wide(w_ref), 1, 1)
    normed = n_ref[...]
    gpre = gh * d_ref[...]
    channels = gpre.shape[1]
    gg_ref[0:1] = jnp.sum(gpre * normed, axis=0, keepdims=True)
    gg_ref[1:2] = jnp.sum(gpre, axis=0, keepdims=True)
    gn = gpre * gain_ref[...]
    m1 = jnp.sum(gn, axis=1, keepdims=True) * (1.0 / channels)
    m2 = jnp.sum(gn * normed, axis=1, keepdims=True) * (1.0 / channels)
    part = (gn - m1 - normed * m2) * i_ref[:, 0:1]
    step = part_ref.shape[2]
    for j in range(part_ref.shape[0]):
        part_ref[j] = part[:, j * step : (j + 1) * step].astype(BF16)


def early_back_a(part_ref, g_ref, b_ref, e_ref, up_ref, pp_ref, gae_ref, gl_ref, gr_ref):
    g = part_ref[0].astype(F32)
    for j in range(1, part_ref.shape[0]):
        g = g + part_ref[j].astype(F32)
    g = g + g_ref[...]
    put_all(gr_ref, excite_back(g, b_ref[...], e_ref, up_ref, gl_ref))
    gae_ref[...] = split_mm(pp_ref[...], g, 0, 0)


def early_back_b(
    size_ref, gr_ref, rpre_ref, down_ref, e_ref, gae_ref, w_ref, gc_ref, grp_ref, part_ref
):
    out = w_ref.shape[2]
    size = size_ref[0].astype(F32)
    gs = squeeze_back(rows_of(gr_ref, gr_ref.shape[0]), rpre_ref, down_ref, grp_ref)
    gs = gs * (1.0 / (size * size + jnp.zeros((1, out), F32)))
    gc = ((gae_ref[...] * e_ref[...] + gs) * size_mask(size_ref[0], out)).astype(BF16)
    gc_ref[...] = gc
    spread = tap_spread(gc.astype(F32), SIDE, out)
    gh = mm(spread, wide(w_ref), 1, 1)
    step = part_ref.shape[2]
    for j in range(part_ref.shape[0]):
        part_ref[j] = gh[:, j * step : (j + 1) * step].astype(BF16)


def early_back_c(
    size_ref, part_ref, x_ref, mom_ref, gain_ref, bias_ref, gn_ref, gg_ref, s_ref
):
    width = x_ref.shape[1]
    gh = part_ref[0].astype(F32)
    for j in range(1, part_ref.shape[0]):
        gh = gh + part_ref[j].astype(F32)
    normed = (x_ref[...] - mom_ref[0]) * mom_ref[1]
    pre = normed * gain_ref[...] + bias_ref[...]
    gpre = gh * size_mask(size_ref[0], width) * silu_grad(pre)
    gg_ref[0:1] = jnp.sum(gpre * normed, axis=0, keepdims=True)
    gg_ref[1:2] = jnp.sum(gpre, axis=0, keepdims=True)
    gn = gpre * gain_ref[...]
    gn_ref[...] = gn
    put_all(s_ref, row_sums(gn, gn * normed))


def early_back_d(channels, size_ref, s_ref, gn_ref, x_ref, mom_ref, gae_ref, fg_ref, low_ref):
    width = x_ref.shape[1]
    acc = rows_of(s_ref, s_ref.shape[0]) * (1.0 / channels)
    m1 = spread_rows(acc, 0, width)
    m2 = spread_rows(acc, 4, width)
    inv = mom_ref[1]
    normed = (x_ref[...] - mom_ref[0]) * inv
    out = (gae_ref[...] + inv * (gn_ref[...] - m1 - normed * m2)) * size_mask(size_ref[0], width)
    fg_ref[...] = out
    low_ref[...] = out.astype(BF16)


def conv_weight_kernel(side, images, slot_ref, h_ref, g_ref, out_ref, gb_ref, spread_ref):
    out = g_ref.shape[2]
    n = side * side

    @pl.when(pl.program_id(0) == 0)
    def _():
        total = None
        for s in range(images):
            g = g_ref[slot_ref[s]].astype(F32)
            one = jnp.sum(g, axis=0, keepdims=True)
            total = one if total is None else total + one
            spread_ref[s * n : (s + 1) * n, :] = tap_spread(g, side, out)
        gb_ref[...] = total

    if len(h_ref.shape) == 4:
        h = jnp.concatenate(
            [
                jnp.concatenate([h_ref[slot_ref[s], j] for j in range(h_ref.shape[1])], axis=1)
                for s in range(images)
            ],
            axis=0,
        )
    else:
        h = jnp.concatenate([h_ref[slot_ref[s]] for s in range(images)], axis=0)
    res = mm(h, spread_ref[...], 0, 0)
    for t in range(9):
        out_ref[t] = res[:, t * out : (t + 1) * out]


def conv_weights(side, slot, h, g, channels, steps):
    images, n, out = g.shape
    rows = channels // steps
    if h.ndim == 4:
        h_spec = pl.BlockSpec(
            (images, h.shape[1] // steps, n, h.shape[3]), lambda k, s: (0, k, 0, 0)
        )
    else:
        h_spec = pl.BlockSpec((images, n, rows), lambda k, s: (0, 0, k))
    return pl.pallas_call(
        partial(conv_weight_kernel, side, images),
        out_shape=[shape((9, channels, out)), shape((1, out))],
        grid_spec=pltpu.PrefetchScalarGridSpec(
            num_scalar_prefetch=1,
            grid=(steps,),
            in_specs=[h_spec, pl.BlockSpec((images, n, out), lambda k, s: (0, 0, 0))],
            out_specs=[
                pl.BlockSpec((9, rows, out), lambda k, s: (0, k, 0)),
                pl.BlockSpec((1, out), lambda k, s: (0, 0)),
            ],
            scratch_shapes=[pltpu.VMEM((images * n, 9 * out), BF16)],
        ),
        cost_estimate=cost(2 * images * n * 9 * out * channels, h.size * 2 + 36 * channels * out),
        name="conv_weights_%d" % side,
    )(slot, h, g)


def dense_weight_kernel(images, slot_ref, a_ref, g_ref, out_ref, gb_ref):
    a = jnp.concatenate([a_ref[slot_ref[s], 0] for s in range(images)], axis=0)
    g = jnp.concatenate([g_ref[slot_ref[s]] for s in range(images)], axis=0)
    out_ref[...] = mm(a, g, 0, 0)

    @pl.when(pl.program_id(0) == 0)
    def _():
        gb_ref[...] = jnp.sum(g.astype(F32), axis=0, keepdims=True)


def dense_weights(slot, a, g):
    images, blocks, rows, width = a.shape
    cols = g.shape[2]
    return pl.pallas_call(
        partial(dense_weight_kernel, images),
        out_shape=[shape((blocks * width, cols)), shape((1, cols))],
        grid_spec=pltpu.PrefetchScalarGridSpec(
            num_scalar_prefetch=1,
            grid=(blocks,),
            in_specs=[
                pl.BlockSpec((images, 1, rows, width), lambda k, s: (0, k, 0, 0)),
                pl.BlockSpec((images, rows, cols), lambda k, s: (0, 0, 0)),
            ],
            out_specs=[
                pl.BlockSpec((width, cols), lambda k, s: (k, 0)),
                pl.BlockSpec((1, cols), lambda k, s: (0, 0)),
            ],
        ),
        cost_estimate=cost(2 * images * rows * blocks * width * cols, a.size * 2 + blocks * width * cols * 4),
        name="dense_weights_%d" % width,
    )(slot, a, g)


def swap(v):
    return lax.all_to_all(v, "mp", 0, 0)


def dp_permute(v, fn):
    n = lax.axis_size("dp")
    return lax.ppermute(v, "dp", [(i, fn(i) % n) for i in range(n)])


def dp_gather(v, relay=True):
    n = lax.axis_size("dp")
    slots = [v, dp_permute(v, lambda i: i ^ 1)]
    for k in range(1, n // 2):
        far = dp_permute(v, lambda i: i + 2 * k)
        slots.append(far)
        if relay:
            slots.append(dp_permute(far, lambda i: i ^ 1))
        else:
            slots.append(dp_permute(v, lambda i: ((i + 2 * k) % n) ^ 1))
    return jnp.stack(slots)


def dp_slots():
    n = lax.axis_size("dp")
    me = lax.axis_index("dp")
    s = jnp.arange(n)
    hops = (me // 2 - s // 2) % (n // 2)
    return (2 * hops + ((s ^ me) & 1)).astype(jnp.int32)


def in_order(stacked, slot):
    return [lax.dynamic_index_in_dim(stacked, slot[s], 0, False) for s in range(stacked.shape[0])]


def row(v):
    return v.reshape(1, -1)


def per_device(
    features,
    position,
    image_sizes,
    gain_early,
    bias_early,
    conv_early,
    conv_bias_early,
    down_early,
    down_bias_early,
    up_early,
    up_bias_early,
    gain_late,
    bias_late,
    conv_late,
    conv_bias_late,
    down_late,
    down_bias_late,
    up_late,
    up_bias_late,
    readout_in,
    readout_in_bias,
    readout_out,
    readout_out_bias,
    out_grad,
):
    mp = lax.axis_size("mp")
    dp = lax.axis_size("dp")
    width = features.shape[0]
    channels = width * mp
    n = SIDE * SIDE
    n2 = GRID * GRID
    se = down_early.shape[1]
    cols = readout_in.shape[1]
    out_cols = readout_out.shape[1]
    slot = dp_slots()

    feats = jnp.transpose(features.reshape(width, n))
    posn = jnp.transpose(position)
    w_early = jnp.transpose(conv_early, (1, 0, 2))
    w_late = jnp.transpose(conv_late, (1, 0, 2))
    pool = jnp.where(
        image_sizes[0] == SIDE, pool_matrix(SIDE, SIDE, GRID), pool_matrix(SMALL, SIDE, GRID)
    )
    pp = (pool[:, None, :, None] * pool[None, :, None, :]).reshape(n2, n).astype(BF16)

    x, sums = call(
        prep_kernel, (shape((n, width)), shape((mp, 8, n))), image_sizes, feats, posn,
        smem=(0,), name="prep",
    )
    late_vec = jnp.broadcast_to(
        jnp.stack([gain_late, bias_late] * 4)[None], (mp, 8, width)
    )
    sums, late_all = swap(jnp.concatenate([sums, late_vec], axis=2)), None
    late_all = sums[:, :2, n:]
    sums = sums[:, :, :n]
    gain_all = late_all[:, 0].reshape(1, channels)
    bias_all = late_all[:, 1].reshape(1, channels)

    hid, mom = call(
        partial(hidden_kernel, channels), (shape((mp, n, width), BF16), shape((2, n, width))),
        image_sizes, x, sums, row(gain_early), row(bias_early), smem=(0,), name="hidden",
    )
    hid = swap(hid)

    gact = pl.pallas_call(
        act_grad_kernel,
        out_shape=shape((mp, n2, cols), BF16),
        grid=(mp,),
        in_specs=[
            pl.BlockSpec((n2, out_cols), lambda j: (0, 0)),
            pl.BlockSpec((cols, out_cols), lambda j: (j, 0)),
        ],
        out_specs=pl.BlockSpec((1, n2, cols), lambda j: (j, 0, 0)),
        cost_estimate=cost(2 * n2 * out_cols * cols * mp, cols * mp * out_cols * 2),
        name="act_grad",
    )(out_grad, readout_out)
    gact = swap(gact)

    conv1, pool_a, pool_b, sq1, rp1 = call(
        conv_kernel,
        (shape((n, width)), shape((n2, width)), shape((n2, width)), shape((1, width)), shape((mp, 8, se))),
        image_sizes, hid, w_early, row(conv_bias_early), x, pp, down_early,
        smem=(0,), flops=2 * n * channels * 9 * width, name="conv",
    )
    rp1 = swap(rp1)
    pooled_own, rpre1, e1 = call(
        pooled_kernel, (shape((mp, n2, width)), shape((1, se)), shape((1, width))),
        rp1, row(down_bias_early), up_early, row(up_bias_early), pool_a, pool_b, name="pooled",
    )
    pooled = swap(pooled_own)

    hid2, conv2, sq2, rp2 = call(
        late_kernel,
        (shape((n2, channels), BF16), shape((n2, width)), shape((1, width)), shape((mp, 8, se))),
        pooled, gain_all, bias_all, w_late, row(conv_bias_late), down_late,
        flops=2 * n2 * channels * 9 * width, name="late",
    )
    rp2 = swap(rp2)
    normed2, inv2, slope2 = call(
        late_slope_kernel,
        (shape((n2, channels)), shape((n2, 128)), shape((n2, channels))),
        pooled, gain_all, bias_all, name="late_slope",
    )
    tok, rpre2, e2 = call(
        token_kernel, (shape((mp, n2, width), BF16), shape((1, se)), shape((1, width))),
        rp2, row(down_bias_late), up_late, row(up_bias_late), pooled_own[0], conv2, name="tokens",
    )
    tok = swap(tok)

    act, gpre, gtok = call(
        readout_kernel,
        (shape((n2, cols), BF16), shape((n2, cols), BF16), shape((mp, n2, width), BF16)),
        tok, readout_in, row(readout_in_bias), gact,
        flops=4 * n2 * channels * cols, name="readout",
    )
    gtok = swap(gtok)
    g2, gl2, gr2 = call(
        late_back_a, (shape((n2, width)), shape((1, width)), shape((mp, 8, se))),
        gtok, conv2, e2, up_late, name="late_back_a",
    )
    gr2 = swap(gr2)
    gconv2, grp2, part2, gg2 = call(
        late_back_b,
        (shape((n2, width), BF16), shape((1, se)), shape((mp, n2, width), BF16), shape((2, channels))),
        gr2, rpre2, down_late, e2, g2, w_late, normed2, inv2, slope2, gain_all,
        flops=2 * n2 * channels * 9 * width, name="late_back_b",
    )
    part2 = swap(part2)
    gae, gl1, gr1 = call(
        early_back_a, (shape((n, width)), shape((1, width)), shape((mp, 8, se))),
        part2, g2, pool_b, e1, up_early, pp, name="early_back_a",
    )
    gg2_blocks = jnp.transpose(gg2.reshape(2, mp, width), (1, 0, 2))
    gg2_blocks = jnp.concatenate([gg2_blocks, jnp.zeros((mp, 6, width), F32)], axis=1)
    mixed = swap(jnp.concatenate([gr1, gg2_blocks], axis=2))
    gr1 = mixed[:, :, :se]
    gg2_own = jnp.sum(mixed[:, 0:2, se:], axis=0)
    gconv1, grp1, part1 = call(
        early_back_b,
        (shape((n, width), BF16), shape((1, se)), shape((mp, n, width), BF16)),
        image_sizes, gr1, rpre1, down_early, e1, gae, w_early,
        smem=(0,), flops=2 * n * channels * 9 * width, name="early_back_b",
    )
    part1 = swap(part1)
    gn1, gg1, gsum = call(
        early_back_c, (shape((n, width)), shape((2, width)), shape((mp, 8, n))),
        image_sizes, part1, x, mom, row(gain_early), row(bias_early), smem=(0,), name="early_back_c",
    )
    gsum = swap(gsum)
    fgrad, fgrad_low = call(
        partial(early_back_d, channels), (shape((n, width)), shape((n, width), BF16)),
        image_sizes, gsum, gn1, x, mom, gae, smem=(0,), name="early_back_d",
    )

    act_all = swap(jnp.broadcast_to(act[None], (mp, n2, cols)))
    tokens_out = pl.pallas_call(
        logits_kernel,
        out_shape=shape((n2, out_cols), BF16),
        grid=(mp,),
        in_specs=[
            pl.BlockSpec((1, n2, cols), lambda j: (j, 0, 0)),
            pl.BlockSpec((cols, out_cols), lambda j: (j, 0)),
            pl.BlockSpec((1, out_cols), lambda j: (0, 0)),
        ],
        out_specs=pl.BlockSpec((n2, out_cols), lambda j: (0, 0)),
        scratch_shapes=[pltpu.VMEM((n2, out_cols), F32)],
        cost_estimate=cost(2 * n2 * out_cols * cols * mp, cols * mp * out_cols * 2),
        name="logits",
    )(act_all, readout_out, row(readout_out_bias))

    grad_out_w, grad_out_b = dense_weights(slot, dp_gather(act_all), dp_gather(out_grad))
    grad_in_w, grad_in_b = dense_weights(slot, dp_gather(tok), dp_gather(gpre))
    grad_w2, grad_cb2 = conv_weights(GRID, slot, dp_gather(hid2), dp_gather(gconv2), channels, 2)
    grad_w1, grad_cb1 = conv_weights(SIDE, slot, dp_gather(hid), dp_gather(gconv1), channels, 2)

    red1 = jax.nn.silu(rpre1[0])
    red2 = jax.nn.silu(rpre2[0])
    vec = jnp.concatenate(
        [red1, red2, grp1[0], grp2[0], gl1[0], gl2[0], sq1[0], sq2[0], gg2_own[0], gg2_own[1]]
    )
    vecs = jnp.stack(in_order(dp_gather(vec, relay=False), slot))
    cuts = [se] * 4 + [width] * 6
    parts = []
    at = 0
    for size in cuts:
        parts.append(vecs[:, at : at + size])
        at += size
    outer = partial(mm, ca=0, cb=0, precision=HI)
    grad_up1 = outer(parts[0], parts[4])
    grad_up2 = outer(parts[1], parts[5])
    grad_down1 = outer(parts[6], parts[2])
    grad_down2 = outer(parts[7], parts[3])
    flat = jnp.sum(vecs[:, 2 * se :], axis=0)
    grad_db1, grad_db2 = flat[:se], flat[se : 2 * se]
    base = 2 * se
    grad_ub1, grad_ub2 = flat[base : base + width], flat[base + width : base + 2 * width]
    base = base + 4 * width
    grad_gain2, grad_bias2 = flat[base : base + width], flat[base + width : base + 2 * width]

    lows = in_order(dp_gather(fgrad_low, relay=False), slot)
    pos_grad = lows[0].astype(F32)
    for one in lows[1:]:
        pos_grad = pos_grad + one.astype(F32)
    ggs = in_order(dp_gather(gg1, relay=False), slot)
    gg1_all = ggs[0]
    for one in ggs[1:]:
        gg1_all = gg1_all + one

    return (
        tokens_out,
        jnp.transpose(fgrad).reshape(width, 1, n),
        jnp.transpose(pos_grad),
        gg1_all[0],
        gg1_all[1],
        jnp.transpose(grad_w1, (1, 0, 2)),
        grad_cb1[0],
        grad_down1,
        grad_db1,
        grad_up1,
        grad_ub1,
        grad_gain2,
        grad_bias2,
        jnp.transpose(grad_w2, (1, 0, 2)),
        grad_cb2[0],
        grad_down2,
        grad_db2,
        grad_up2,
        grad_ub2,
        grad_in_w,
        grad_in_b[0],
        grad_out_w,
        grad_out_b[0],
    )


def solution(mesh):
    by_mp = P("mp")
    block = (by_mp, by_mp, P(None, None, "mp"), by_mp, P("mp", None), P(), P(None, "mp"), by_mp)
    return jax.shard_map(
        per_device,
        mesh=mesh,
        in_specs=(P("mp", "dp", None), P("mp", None), P("dp"))
        + block
        + block
        + (P(None, "mp"), by_mp, P(None, "mp"), by_mp, P("dp", "mp")),
        out_specs=(P("dp", "mp"), P("mp", "dp", None), P("mp", None))
        + block
        + block
        + (P(None, "mp"), by_mp, P(None, "mp"), by_mp),
        check_vma=False,
    )
```

```python
from functools import partial

import jax
import jax.numpy as jnp
from jax import lax
from jax.experimental import pallas as pl
from jax.experimental.pallas import tpu as pltpu
from jax.sharding import PartitionSpec as P

SIDE = 24
SMALL = 16
GRID = 12
EPS = 1e-06
F32 = jnp.float32
BF16 = jnp.bfloat16
HI = lax.Precision.HIGHEST


def pool_matrix(extent, side_len, grid_len):
    row_index = jnp.arange(grid_len)[:, None]
    col_index = jnp.arange(side_len)[None, :]
    first_col = row_index * extent // grid_len
    end_col = -(-(row_index + 1) * extent // grid_len)
    in_bin = (col_index >= first_col) & (col_index < end_col)
    return jnp.where(in_bin, 1.0, 0.0).astype(F32) / (end_col - first_col).astype(F32)


def shape(dims, dtype=F32):
    return jax.ShapeDtypeStruct(dims, dtype)


def cost(flops, nbytes):
    return pl.CostEstimate(flops=int(flops), bytes_accessed=int(nbytes), transcendentals=0)


def call(kernel, outs, *args, flops=1e6, smem=(), name=None):
    specs = [
        pl.BlockSpec(memory_space=pltpu.SMEM if k in smem else pltpu.VMEM)
        for k in range(len(args))
    ]
    nbytes = sum(a.size * a.dtype.itemsize for a in args) + sum(
        o.size * jnp.dtype(o.dtype).itemsize for o in outs
    )
    return pl.pallas_call(
        kernel,
        out_shape=list(outs),
        in_specs=specs,
        out_specs=[pl.BlockSpec(memory_space=pltpu.VMEM) for _ in outs],
        cost_estimate=cost(flops, nbytes),
        name=name,
    )(*args)


def mm(a, b, ca, cb, precision=None):
    return lax.dot_general(
        a, b, (((ca,), (cb,)), ((), ())), preferred_element_type=F32, precision=precision
    )


def sigmoid(v):
    return 1.0 / (1.0 + jnp.exp(-v))


def silu_grad(v):
    s = sigmoid(v)
    return s * (1.0 + v * (1.0 - s))


def grid_rc(side, lanes):
    i = lax.broadcasted_iota(jnp.int32, (side * side, lanes), 0).astype(F32)
    r = jnp.floor((i + 0.5) * (1.0 / side))
    return r, i - r * side


def tap_ok(r, c, side, dy, dx):
    ok = None
    for v, d in ((r, dy), (c, dx)):
        if d == 0:
            continue
        one = (v >= 0.5) if d < 0 else (v <= side - 1.5)
        ok = one if ok is None else ok & one
    return ok


def tap_sum(y, side, width):
    n = side * side
    r, c = grid_rc(side, width)
    total = None
    for t in range(9):
        dy, dx = t // 3 - 1, t % 3 - 1
        part = y[:, t * width : (t + 1) * width]
        off = dy * side + dx
        if off:
            part = pltpu.roll(part, (-off) % n, 0)
        ok = tap_ok(r, c, side, dy, dx)
        if ok is not None:
            part = jnp.where(ok, part, 0.0)
        total = part if total is None else total + part
    return total


def tap_spread(g, side, width):
    n = side * side
    r, c = grid_rc(side, width)
    parts = []
    for t in range(9):
        dy, dx = t // 3 - 1, t % 3 - 1
        off = dy * side + dx
        part = pltpu.roll(g, off % n, 0) if off else g
        ok = tap_ok(r, c, side, -dy, -dx)
        if ok is not None:
            part = jnp.where(ok, part, 0.0)
        parts.append(part.astype(BF16))
    return jnp.concatenate(parts, axis=1)


def wide(ref):
    return jnp.concatenate([ref[j] for j in range(ref.shape[0])], axis=1)


def split_mm(p, v, ca, cb):
    top = v.astype(BF16)
    low = (v - top.astype(F32)).astype(BF16)
    return mm(p, top, ca, cb) + mm(p, low, ca, cb)


def size_mask(size, width):
    r, c = grid_rc(SIDE, width)
    s = size.astype(F32) - 0.5
    return jnp.where((r < s) & (c < s), 1.0, 0.0).astype(F32)


def put_all(ref, value):
    for j in range(ref.shape[0]):
        ref[j] = value


def pieces_of(v, count):
    out = []
    for _ in range(count):
        top = v.astype(BF16).astype(F32)
        out.append(top)
        v = v - top
    return out


def tail_rows(total):
    return -(-total // 16) * 16


def pack(rows, width):
    height = tail_rows(len(rows))
    index = lax.broadcasted_iota(jnp.int32, (height, width), 0)
    out = jnp.zeros((height, width), F32)
    for k, one in enumerate(rows):
        out = jnp.where(index == k, one, out)
    return out.astype(BF16)


def chop(v, width):
    return [
        p[:, k * width : (k + 1) * width]
        for p in pieces_of(v, 3)
        for k in range(v.shape[1] // width)
    ]


def join(acc, first, length):
    k = length // acc.shape[1]
    rows = [acc[first + i : first + i + 1] for i in range(3 * k)]
    return jnp.concatenate([rows[i] + rows[k + i] + rows[2 * k + i] for i in range(k)], axis=1)


def plain_join(acc, length):
    k = length // acc.shape[1]
    return jnp.concatenate([acc[i : i + 1] for i in range(k)], axis=1)


def block_sum(ref, first, last):
    acc = ref[0, first:last, :].astype(F32)
    for j in range(1, ref.shape[0]):
        acc = acc + ref[j, first:last, :].astype(F32)
    return acc


def wide_rows(ref, first, last):
    return jnp.concatenate([ref[j, first:last, :] for j in range(ref.shape[0])], axis=1)


def two_mm(v, w, cb):
    top, low = pieces_of(jnp.broadcast_to(v, (8, v.shape[1])), 2)
    return (mm(top.astype(BF16), w, 1, cb) + mm(low.astype(BF16), w, 1, cb))[0:1]


def small_mm(v, w, cb):
    return mm(jnp.broadcast_to(v, (8, v.shape[1])), w, 1, cb, HI)[0:1]


def per_side(size, width):
    size = size.astype(F32)
    return 1.0 / (size * size + jnp.zeros((1, width), F32))


def silu(v):
    return v * sigmoid(v)


def flat_rows(v, width):
    return [v[:, k * width : (k + 1) * width] for k in range(v.shape[1] // width)]


def pack32(rows, width):
    height = -(-len(rows) // 8) * 8
    index = lax.broadcasted_iota(jnp.int32, (height, width), 0)
    out = jnp.zeros((height, width), F32)
    for k, one in enumerate(rows):
        out = jnp.where(index == k, one, out)
    return out


def lead_rows(n, width):
    return tail_rows(12 + -(-n // width))


def prep_kernel(place_ref, size_ref, f_ref, p_ref, up1_ref, up2_ref, *rest):
    vec_refs, out_ref = rest[:-1], rest[-1]
    n, width = f_ref.shape
    x = (f_ref[...].astype(F32) + p_ref[...].astype(F32)) * size_mask(size_ref[0], width)
    middle = (jnp.sum(x, axis=1, keepdims=True) * (1.0 / width)).astype(BF16).astype(F32)
    lane = lax.broadcasted_iota(jnp.int32, (n, width), 1)
    line = mm(jnp.ones((8, width), F32), jnp.where(lane == 0, middle, 0.0), 1, 1)[0:1]
    count = -(-n // width)
    if count * width > n:
        line = jnp.concatenate([line, jnp.zeros((1, count * width - n), F32)], axis=1)
    rows = []
    for ref in vec_refs:
        rows += pieces_of(ref[...], 2)
    rows += flat_rows(line, width)
    part = (out_ref.shape[1] - n - tail_rows(len(rows))) // 2
    start = pl.multiple_of(place_ref[0] * part, part)
    up = [r[pl.ds(start, part), :].astype(BF16) for r in (up1_ref, up2_ref)]
    value = jnp.concatenate([(x - middle).astype(BF16), pack(rows, width)] + up, axis=0)
    put_all(out_ref, value)


def lead_of(x_ref, n):
    width = x_ref.shape[2]
    return [x_ref[j, n : n + lead_rows(n, width), :].astype(F32) for j in range(x_ref.shape[0])]


def restore_x(x_ref, lead, n):
    blocks, _, width = x_ref.shape
    count = -(-n // width)
    lines = [
        jnp.concatenate([p[12 + k : 13 + k] for k in range(count)], axis=1)[:, :n] for p in lead
    ]
    lines = jnp.concatenate(lines, axis=0)
    shape2 = (blocks, blocks * width)
    col = lax.broadcasted_iota(jnp.int32, shape2, 1).astype(F32)
    home = lax.broadcasted_iota(jnp.int32, shape2, 0).astype(F32)
    here = jnp.floor((col + 0.5) * (1.0 / width)) == home
    spread = mm(lines, jnp.where(here, 1.0, 0.0).astype(F32), 0, 0)
    return wide_rows(x_ref, 0, n).astype(F32) + spread


def unpack_up_kernel(images, slot_ref, *refs):
    parts, (up1_ref, up2_ref, buf_ref, sems) = refs[:images], refs[images:]
    fetch(slot_ref, parts, buf_ref, sems, whole_ref)
    arrive(parts, buf_ref, sems, whole_ref)
    q = buf_ref.shape[2] // 2
    for s in range(images):
        both = jnp.concatenate([buf_ref[s, j] for j in range(buf_ref.shape[1])], axis=1)
        up1_ref[s * q : (s + 1) * q, :] = both[:q]
        up2_ref[s * q : (s + 1) * q, :] = both[q:]


def unpack_up(slot, parts, se, channels):
    images = len(parts)
    return pl.pallas_call(
        partial(unpack_up_kernel, images),
        out_shape=[shape((se, channels), BF16), shape((se, channels), BF16)],
        in_specs=[pl.BlockSpec(memory_space=pltpu.SMEM)] + any_specs(images),
        out_specs=[pl.BlockSpec(memory_space=pltpu.VMEM)] * 2,
        scratch_shapes=[
            pltpu.VMEM((images,) + parts[0].shape, BF16), pltpu.SemaphoreType.DMA((images,))
        ],
        cost_estimate=cost(1e6, 2e6),
        name="unpack_up",
    )(slot, *parts)


def norm_rows(x, gain, bias):
    scale = 1.0 / x.shape[1]
    center = jnp.sum(x, axis=1, keepdims=True) * scale
    d = x - center
    inv = lax.rsqrt(jnp.sum(d * d, axis=1, keepdims=True) * scale + EPS)
    normed = d * inv
    return normed, inv, normed * gain + bias


def front_kernel(
    size_ref, x_ref, w_ref, cb_ref, pp_ref, down_ref, vec_ref, h_ref, pay_ref, a_ref, b_ref, sq_ref
):
    out = w_ref.shape[2]
    blocks = x_ref.shape[0]
    n = SIDE * SIDE
    packed = lead_of(x_ref, n)
    x = restore_x(x_ref, packed, n)
    a_ref[...] = split_mm(pp_ref[...], x, 1, 0)
    for k in range(6):
        vec_ref[k : k + 1] = jnp.concatenate(
            [p[2 * k : 2 * k + 1] + p[2 * k + 1 : 2 * k + 2] for p in packed], axis=1
        )
    vec_ref[6:8] = jnp.zeros((2, vec_ref.shape[1]), F32)
    _, _, pre = norm_rows(x, vec_ref[0:1], vec_ref[1:2])
    mask = size_mask(size_ref[0], out)
    h = (silu(pre) * jnp.concatenate([mask] * blocks, axis=1)).astype(BF16)
    h_ref[...] = h
    y = mm(h, wide(w_ref), 1, 0)
    conv = (tap_sum(y, SIDE, out) + cb_ref[...]) * mask
    pooled = split_mm(pp_ref[...], conv, 1, 0)
    b_ref[...] = pooled
    sq = jnp.sum(conv, axis=0, keepdims=True) * per_side(size_ref[0], out)
    sq_ref[...] = sq
    tail = pack32(flat_rows(small_mm(sq, down_ref[...], 0), out), out)
    put_all(pay_ref, jnp.concatenate([pooled, tail], axis=0))


def early_slope_kernel(size_ref, x_ref, vec_ref, n_ref, i_ref, d_ref):
    blocks, _, width = x_ref.shape
    x = restore_x(x_ref, lead_of(x_ref, SIDE * SIDE), SIDE * SIDE)
    normed, inv, pre = norm_rows(x, vec_ref[0:1], vec_ref[1:2])
    n_ref[...] = normed
    i_ref[...] = jnp.broadcast_to(inv, i_ref.shape)
    mask = size_mask(size_ref[0], width)
    d_ref[...] = silu_grad(pre) * jnp.concatenate([mask] * blocks, axis=1)


def late_kernel(
    ball_ref, a_ref, up_all_ref, db_ref, vec_ref, up_ref, ub_ref, w_ref, cb_ref, down_ref,
    h_ref, pool_ref, pay_ref, conv_ref, sq_ref, rpre_ref, e_ref, eall_ref,
):
    out = w_ref.shape[2]
    n = GRID * GRID
    rpre = plain_join(block_sum(ball_ref, n, ball_ref.shape[1]), db_ref.shape[1]) + db_ref[...]
    rpre_ref[...] = rpre
    red = silu(rpre)
    e_all = sigmoid(two_mm(red, up_all_ref[...], 0) + vec_ref[4:5])
    eall_ref[...] = e_all
    e_ref[...] = sigmoid(small_mm(red, up_ref[...], 0) + ub_ref[...])
    pooled = a_ref[...] + wide_rows(ball_ref, 0, n) * e_all
    pool_ref[...] = pooled
    _, _, pre = norm_rows(pooled, vec_ref[2:3], vec_ref[3:4])
    h = silu(pre).astype(BF16)
    h_ref[...] = h
    y = mm(h, wide(w_ref), 1, 0)
    conv = tap_sum(y, GRID, out) + cb_ref[...]
    conv_ref[...] = conv
    sq = jnp.sum(conv, axis=0, keepdims=True) * (1.0 / n)
    sq_ref[...] = sq
    tail = pack32(flat_rows(small_mm(sq, down_ref[...], 0), out), out)
    put_all(pay_ref, jnp.concatenate([conv, tail], axis=0))


def late_slope_kernel(pool_ref, vec_ref, n_ref, i_ref, d_ref):
    normed, inv, pre = norm_rows(pool_ref[...], vec_ref[2:3], vec_ref[3:4])
    n_ref[...] = normed
    i_ref[...] = jnp.broadcast_to(inv, i_ref.shape)
    d_ref[...] = silu_grad(pre)


def put_blocks(ref, values, tails):
    step = ref.shape[2]
    for j in range(ref.shape[0]):
        tail = tails if not isinstance(tails, list) else tails[j]
        block = values[:, j * step : (j + 1) * step].astype(BF16)
        ref[j] = jnp.concatenate([block, tail], axis=0)


def readout_kernel(
    call_ref, pool_ref, up_all_ref, db_ref, vec_ref, up_ref, ub_ref, w_ref, b_ref, *rest
):
    gh_refs = rest[:-7]
    t_ref, act_ref, gp_ref, pay_ref, rpre_ref, e_ref, spare_ref = rest[-7:]
    n = GRID * GRID
    width = pay_ref.shape[2]
    rpre = plain_join(block_sum(call_ref, n, call_ref.shape[1]), db_ref.shape[1]) + db_ref[...]
    rpre_ref[...] = rpre
    red = silu(rpre)
    e_all = sigmoid(two_mm(red, up_all_ref[...], 0) + vec_ref[5:6])
    spare_ref[...] = e_all
    e_ref[...] = sigmoid(small_mm(red, up_ref[...], 0) + ub_ref[...])
    conv = wide_rows(call_ref, 0, n)
    tok = (pool_ref[...] + conv * e_all).astype(BF16)
    t_ref[...] = tok
    pre = mm(tok, w_ref[...], 1, 0) + b_ref[...]
    phi = 0.5 * (1.0 + lax.erf(pre * 0.7071067811865476))
    act_ref[...] = (pre * phi).astype(BF16)
    dens = 0.3989422804014327 * jnp.exp(-0.5 * pre * pre)
    gh = gh_refs[0][...].astype(F32)
    for one in gh_refs[1:]:
        gh = gh + one[...].astype(F32)
    gp = (gh * (phi + pre * dens)).astype(BF16)
    gp_ref[...] = gp
    gt = mm(gp, w_ref[...], 1, 1)
    gl = jnp.sum(gt * conv, axis=0, keepdims=True) * e_all * (1.0 - e_all)
    put_blocks(pay_ref, gt, pack(chop(two_mm(gl, up_all_ref[...], 1), width), width))


def act_grad_kernel(order_ref, g_ref, w_ref, out_ref):
    out_ref[0] = mm(g_ref[...], w_ref[...], 1, 1).astype(BF16)


def logits_kernel(blocks_ref, a0_ref, a1_ref, w_ref, b_ref, out_ref, acc_ref):
    j = pl.program_id(0)
    half = pl.num_programs(0) // 2

    @pl.when(j == 0)
    def _():
        acc_ref[...] = jnp.zeros_like(acc_ref)

    @pl.when(j < half)
    def _():
        acc_ref[...] += mm(a0_ref[0], w_ref[...], 1, 0)

    @pl.when(j >= half)
    def _():
        acc_ref[...] += mm(a1_ref[0], w_ref[...], 1, 0)

    @pl.when(j == pl.num_programs(0) - 1)
    def _():
        out_ref[...] = (acc_ref[...] + b_ref[...]).astype(BF16)


def squeeze_back(gr, rpre_ref, down_ref, grp_ref):
    grp = gr * silu_grad(rpre_ref[...])
    grp_ref[...] = grp
    return small_mm(grp, down_ref[...], 1)


def norm_back(gh, d_ref, n_ref, i_ref, gain):
    normed = n_ref[...]
    gpre = gh * d_ref[...]
    scale = 1.0 / gh.shape[1]
    g_gain = jnp.sum(gpre * normed, axis=0, keepdims=True)
    g_bias = jnp.sum(gpre, axis=0, keepdims=True)
    gn = gpre * gain
    m1 = jnp.sum(gn, axis=1, keepdims=True) * scale
    m2 = jnp.sum(gn * normed, axis=1, keepdims=True) * scale
    return (gn - m1 - normed * m2) * i_ref[:, 0:1], g_gain, g_bias


def gain_tails(extra, g_gain, g_bias, width, blocks):
    tails = []
    for j in range(blocks):
        rows = list(extra)
        for v in (g_gain, g_bias):
            rows += pieces_of(v[:, j * width : (j + 1) * width], 3)
        tails.append(pack(rows, width))
    return tails


def late_back_kernel(
    me_ref, gt_ref, conv_ref, e_ref, rpre_ref, down_ref, w_ref, n_ref, i_ref, d_ref, vec_ref,
    ball_ref, eall_ref, up_all_ref, gc_ref, grp_ref, gl_ref, pay_ref,
):
    out = w_ref.shape[2]
    blocks = pay_ref.shape[0]
    n = GRID * GRID
    se = rpre_ref.shape[1]
    g = block_sum(gt_ref, 0, n)
    e = e_ref[...]
    gl_ref[...] = jnp.sum(g * conv_ref[...], axis=0, keepdims=True) * e * (1.0 - e)
    gr = join(block_sum(gt_ref, n, gt_ref.shape[1]), 0, se)
    gs = squeeze_back(gr, rpre_ref, down_ref, grp_ref)
    gc = (g * e + gs * (1.0 / n)).astype(BF16)
    gc_ref[...] = gc
    gh = mm(tap_spread(gc.astype(F32), GRID, out), wide(w_ref), 1, 1)
    part, g_gain, g_bias = norm_back(gh, d_ref, n_ref, i_ref, vec_ref[2:3])
    own = [g * jnp.where(me_ref[0] == j, 1.0, 0.0).astype(F32) for j in range(blocks)]
    part = part + jnp.concatenate(own, axis=1)
    e_all = eall_ref[...]
    pooled = wide_rows(ball_ref, 0, n)
    gl1 = jnp.sum(part * pooled, axis=0, keepdims=True) * e_all * (1.0 - e_all)
    extra = chop(two_mm(gl1, up_all_ref[...], 1), out)
    put_blocks(pay_ref, part, gain_tails(extra, g_gain, g_bias, out, blocks))


def early_back_kernel(
    size_ref, p2_ref, b_ref, e_ref, rpre_ref, down_ref, pp_ref, w_ref, n_ref, i_ref, d_ref, vec_ref,
    gae_ref, gc_ref, grp_ref, gl_ref, gg_ref, pay_ref,
):
    out = w_ref.shape[2]
    blocks = pay_ref.shape[0]
    n2 = GRID * GRID
    se = rpre_ref.shape[1]
    g = block_sum(p2_ref, 0, n2)
    tail = block_sum(p2_ref, n2, p2_ref.shape[1])
    e = e_ref[...]
    gl_ref[...] = jnp.sum(g * b_ref[...], axis=0, keepdims=True) * e * (1.0 - e)
    used = 3 * (se // out)
    gg_ref[0:1] = join(tail, used, out)
    gg_ref[1:2] = join(tail, used + 3, out)
    gs = squeeze_back(join(tail, 0, se), rpre_ref, down_ref, grp_ref) * per_side(size_ref[0], out)
    gae = split_mm(pp_ref[...], g, 0, 0)
    gae_ref[...] = gae
    gc = ((gae * e + gs) * size_mask(size_ref[0], out)).astype(BF16)
    gc_ref[...] = gc
    gh = mm(tap_spread(gc.astype(F32), SIDE, out), wide(w_ref), 1, 1)
    part, g_gain, g_bias = norm_back(gh, d_ref, n_ref, i_ref, vec_ref[0:1])
    put_blocks(pay_ref, part, gain_tails([], g_gain, g_bias, out, blocks))


def final_kernel(size_ref, p1_ref, gae_ref, fg_ref, low_ref):
    n, width = gae_ref.shape
    out = (gae_ref[...] + block_sum(p1_ref, 0, n)) * size_mask(size_ref[0], width)
    fg_ref[...] = out
    tail = block_sum(p1_ref, n, p1_ref.shape[1])
    rows = []
    for k in range(2):
        rows += pieces_of(join(tail, 3 * k, width), 3)
    low_ref[...] = jnp.concatenate([out.astype(BF16), pack(rows, width)], axis=0)


def fetch(slot_ref, refs, dst_ref, sems, pick):
    for s in range(len(refs)):
        for q, ref in enumerate(refs):

            @pl.when(slot_ref[s] == q)
            def _():
                pltpu.make_async_copy(pick(ref), dst_ref.at[s], sems.at[s]).start()


def arrive(refs, dst_ref, sems, pick):
    for s in range(len(refs)):
        pltpu.make_async_copy(pick(refs[0]), dst_ref.at[s], sems.at[s]).wait()


def any_specs(count):
    return [pl.BlockSpec(memory_space=pl.ANY)] * count


def whole_ref(ref):
    return ref


def position_kernel(images, slot_ref, *refs):
    lows, (pos_ref, gg_ref, buf_ref, sems) = refs[:images], refs[images:]
    fetch(slot_ref, lows, buf_ref, sems, whole_ref)
    arrive(lows, buf_ref, sems, whole_ref)
    n = pos_ref.shape[0]
    acc = buf_ref[0].astype(F32)
    for s in range(1, images):
        acc = acc + buf_ref[s].astype(F32)
    pos_ref[...] = acc[:n]
    for k in range(2):
        gg_ref[k : k + 1] = join(acc[n:], 3 * k, acc.shape[1])


def position_sum(slot, lows):
    images = len(lows)
    tall, width = lows[0].shape
    n = SIDE * SIDE
    return pl.pallas_call(
        partial(position_kernel, images),
        out_shape=[shape((n, width)), shape((2, width))],
        in_specs=[pl.BlockSpec(memory_space=pltpu.SMEM)] + any_specs(images),
        out_specs=[pl.BlockSpec(memory_space=pltpu.VMEM)] * 2,
        scratch_shapes=[
            pltpu.VMEM((images, tall, width), BF16), pltpu.SemaphoreType.DMA((images,))
        ],
        cost_estimate=cost(1e6, images * tall * width * 2),
        name="position",
    )(slot, *lows)


def parcel_kernel(g1_ref, g2_ref, *refs):
    vecs, out_ref = refs[:-1], refs[-1]
    width = out_ref.shape[1]
    rows = []
    for ref in vecs[:2]:
        rows += chop(silu(ref[...]), width)
    for ref in vecs[2:8]:
        rows += chop(ref[...], width)
    rows += chop(vecs[8][0:1], width) + chop(vecs[8][1:2], width)
    out_ref[...] = jnp.concatenate([g1_ref[...], g2_ref[...], pack(rows, width)], axis=0)


def small_kernel(images, se, slot_ref, *refs):
    parcels = refs[:images]
    d1_ref, u1_ref, d2_ref, u2_ref, flat_ref, wide_ref, buf_ref, sems = refs[images:]
    first = SIDE * SIDE + GRID * GRID
    count = buf_ref.shape[1]

    def pick(ref):
        return ref.at[pl.ds(first, count), :]

    fetch(slot_ref, parcels, buf_ref, sems, pick)
    arrive(parcels, buf_ref, sems, pick)
    width = buf_ref.shape[2]
    lengths = [se] * 4 + [width] * 6
    tables = []
    at = 0
    tails = [buf_ref[s].astype(F32) for s in range(images)]
    for length in lengths:
        index = lax.broadcasted_iota(jnp.int32, (8, length), 0)
        table = jnp.zeros((8, length), F32)
        for s in range(images):
            table = jnp.where(index == s, join(tails[s], at, length), table)
        tables.append(table)
        at += 3 * (length // width)
    u1_ref[...] = mm(tables[0], tables[4], 0, 0, HI)
    u2_ref[...] = mm(tables[1], tables[5], 0, 0, HI)
    d1_ref[...] = mm(tables[6], tables[2], 0, 0, HI)
    d2_ref[...] = mm(tables[7], tables[3], 0, 0, HI)
    for k, table in enumerate(tables[2:4]):
        flat_ref[k : k + 1] = jnp.sum(table, axis=0, keepdims=True)
    for k, t in enumerate((4, 5, 8, 9)):
        wide_ref[k : k + 1] = jnp.sum(tables[t], axis=0, keepdims=True)


def small_grads(slot, parcels, se):
    images = len(parcels)
    tall, width = parcels[0].shape
    outs = [(width, se), (se, width), (width, se), (se, width), (2, se), (4, width)]
    return pl.pallas_call(
        partial(small_kernel, images, se),
        out_shape=[shape(o) for o in outs],
        in_specs=[pl.BlockSpec(memory_space=pltpu.SMEM)] + any_specs(images),
        out_specs=[pl.BlockSpec(memory_space=pltpu.VMEM)] * 6,
        scratch_shapes=[
            pltpu.VMEM((images, tall - SIDE * SIDE - GRID * GRID, width), BF16),
            pltpu.SemaphoreType.DMA((images,)),
        ],
        cost_estimate=cost(1e6, 1e6),
        name="small_grads",
    )(slot, *parcels)


def spread_all(images, side, g_ref, spread_ref, gb_ref):
    n = side * side
    total = None
    for s in range(images):
        g = g_ref[s].astype(F32)
        one = jnp.sum(g, axis=0, keepdims=True)
        total = one if total is None else total + one
        spread_ref[s * n : (s + 1) * n, :] = tap_spread(g, side, g.shape[1])
    gb_ref[...] = total


def early_weight_kernel(images, slot_ref, *refs):
    hids, parcels = refs[:images], refs[images : 2 * images]
    out_ref, gb_ref, h_ref, g_ref, spread_ref, sems, sems2 = refs[2 * images :]
    n = SIDE * SIDE
    out = g_ref.shape[2]
    step = pl.program_id(0)
    width = out_ref.shape[1]

    def pick(ref):
        return ref.at[pl.ds(0, n), :]

    @pl.when(step == 0)
    def _():
        fetch(slot_ref, parcels, g_ref, sems2, pick)
        fetch(slot_ref, hids, h_ref, sems, whole_ref)
        arrive(parcels, g_ref, sems2, pick)
        spread_all(images, SIDE, g_ref, spread_ref, gb_ref)
        arrive(hids, h_ref, sems, whole_ref)

    lanes = pl.ds(pl.multiple_of(step * width, width), width)
    h = jnp.concatenate([h_ref[s, :, lanes] for s in range(images)], axis=0)
    res = mm(h, spread_ref[...], 0, 0)
    for t in range(9):
        out_ref[t] = res[:, t * out : (t + 1) * out]


def early_weights(slot, hids, parcels, steps):
    images = len(hids)
    n, channels = hids[0].shape
    out = parcels[0].shape[1]
    rows = channels // steps
    return pl.pallas_call(
        partial(early_weight_kernel, images),
        out_shape=[shape((9, channels, out)), shape((1, out))],
        grid_spec=pltpu.PrefetchScalarGridSpec(
            num_scalar_prefetch=1,
            grid=(steps,),
            in_specs=any_specs(2 * images),
            out_specs=[
                pl.BlockSpec((9, rows, out), lambda k, s: (0, k, 0)),
                pl.BlockSpec((1, out), lambda k, s: (0, 0)),
            ],
            scratch_shapes=[
                pltpu.VMEM((images, n, channels), BF16),
                pltpu.VMEM((images, n, out), BF16),
                pltpu.VMEM((images * n, 9 * out), BF16),
                pltpu.SemaphoreType.DMA((images,)),
                pltpu.SemaphoreType.DMA((images,)),
            ],
        ),
        cost_estimate=cost(
            2 * images * n * 9 * out * channels, images * n * channels * 2 + 36 * channels * out
        ),
        name="early_weights",
    )(slot, *hids, *parcels)


def late_weight_kernel(images, channels, cols, slot_ref, *refs):
    cats, parcels = refs[:images], refs[images : 2 * images]
    w_ref, gb_ref, in_ref, ib_ref, c_ref, g_ref, spread_ref, sems, sems2 = refs[2 * images :]
    n = GRID * GRID
    out = g_ref.shape[2]
    step = pl.program_id(0)
    width = w_ref.shape[1]

    def pick_cat(ref):
        return ref.at[:, pl.ds(0, c_ref.shape[2])]

    def pick(ref):
        return ref.at[pl.ds(SIDE * SIDE, n), :]

    @pl.when(step == 0)
    def _():
        fetch(slot_ref, parcels, g_ref, sems2, pick)
        fetch(slot_ref, cats, c_ref, sems, pick_cat)
        arrive(parcels, g_ref, sems2, pick)
        spread_all(images, GRID, g_ref, spread_ref, gb_ref)
        arrive(cats, c_ref, sems, pick_cat)

    gp = jnp.concatenate([c_ref[s, :, 2 * channels :] for s in range(images)], axis=0)

    @pl.when(step == 0)
    def _():
        ib_ref[...] = jnp.sum(gp.astype(F32), axis=0, keepdims=True)

    lanes = pl.ds(pl.multiple_of(step * width, width), width)
    tok = jnp.concatenate([c_ref[s, :, lanes] for s in range(images)], axis=0)
    in_ref[...] = mm(tok, gp, 0, 0)
    lanes = pl.ds(pl.multiple_of(step * width + channels, width), width)
    h = jnp.concatenate([c_ref[s, :, lanes] for s in range(images)], axis=0)
    res = mm(h, spread_ref[...], 0, 0)
    for t in range(9):
        w_ref[t] = res[:, t * out : (t + 1) * out]


def late_weights(slot, cats, parcels, channels, cols, steps):
    images = len(cats)
    n = cats[0].shape[0]
    out = parcels[0].shape[1]
    rows = channels // steps
    return pl.pallas_call(
        partial(late_weight_kernel, images, channels, cols),
        out_shape=[
            shape((9, channels, out)), shape((1, out)), shape((channels, cols)), shape((1, cols))
        ],
        grid_spec=pltpu.PrefetchScalarGridSpec(
            num_scalar_prefetch=1,
            grid=(steps,),
            in_specs=any_specs(2 * images),
            out_specs=[
                pl.BlockSpec((9, rows, out), lambda k, s: (0, k, 0)),
                pl.BlockSpec((1, out), lambda k, s: (0, 0)),
                pl.BlockSpec((rows, cols), lambda k, s: (k, 0)),
                pl.BlockSpec((1, cols), lambda k, s: (0, 0)),
            ],
            scratch_shapes=[
                pltpu.VMEM((images, n, 2 * channels + cols), BF16),
                pltpu.VMEM((images, n, out), BF16),
                pltpu.VMEM((images * n, 9 * out), BF16),
                pltpu.SemaphoreType.DMA((images,)),
                pltpu.SemaphoreType.DMA((images,)),
            ],
        ),
        cost_estimate=cost(2 * images * n * (9 * out + cols) * channels, 12e6),
        name="late_weights",
    )(slot, *cats, *parcels)


def act_weight_kernel(images, offset, slot_ref, blocks_ref, *refs):
    act0, act1, cats = (refs[k * images : (k + 1) * images] for k in range(3))
    out_ref, gb_ref, a_ref, g_ref, sems0, sems1, sems2 = refs[3 * images :]
    j = pl.program_id(0)
    half = pl.num_programs(0) // 2

    def pick(ref):
        return ref.at[:, pl.ds(offset, g_ref.shape[2])]

    @pl.when(j == 0)
    def _():
        fetch(slot_ref, cats, g_ref, sems2, pick)
        fetch(slot_ref, act0, a_ref.at[0], sems0, whole_ref)
        fetch(slot_ref, act1, a_ref.at[1], sems1, whole_ref)
        arrive(cats, g_ref, sems2, pick)
        arrive(act0, a_ref.at[0], sems0, whole_ref)

    @pl.when(j == half)
    def _():
        arrive(act1, a_ref.at[1], sems1, whole_ref)

    g = jnp.concatenate([g_ref[s] for s in range(images)], axis=0)

    @pl.when(j == 0)
    def _():
        gb_ref[...] = jnp.sum(g.astype(F32), axis=0, keepdims=True)

    side = j // half
    k = j % half
    a = jnp.concatenate([a_ref[side, s, k] for s in range(images)], axis=0)
    out_ref[...] = mm(a, g, 0, 0)


def act_weights(slot, blocks, act0, act1, cats, offset, cols):
    images = len(act0)
    half, rows, width = act0[0].shape
    total = 2 * half
    return pl.pallas_call(
        partial(act_weight_kernel, images, offset),
        out_shape=[shape((total * width, cols)), shape((1, cols))],
        grid_spec=pltpu.PrefetchScalarGridSpec(
            num_scalar_prefetch=2,
            grid=(total,),
            in_specs=any_specs(3 * images),
            out_specs=[
                pl.BlockSpec((width, cols), lambda k, s, b: (b[k], 0)),
                pl.BlockSpec((1, cols), lambda k, s, b: (0, 0)),
            ],
            scratch_shapes=[
                pltpu.VMEM((2, images, half, rows, width), BF16),
                pltpu.VMEM((images, rows, cols), BF16),
            ]
            + [pltpu.SemaphoreType.DMA((images,))] * 3,
        ),
        cost_estimate=cost(
            2 * images * rows * total * width * cols, images * total * rows * width * 2 + total * width * cols * 4
        ),
        name="act_weights",
    )(slot, blocks, *act0, *act1, *cats)


def swap(v):
    return lax.all_to_all(v, "mp", 0, 0)


def permute(v, axis, fn):
    n = lax.axis_size(axis)
    return lax.ppermute(v, axis, [(i, fn(i) % n) for i in range(n)])


def dp_gather(v, relay=True):
    n = lax.axis_size("dp")
    slots = [v, permute(v, "dp", lambda i: i ^ 1)]
    for k in range(1, n // 2):
        far = permute(v, "dp", lambda i: i + 2 * k)
        slots.append(far)
        if relay:
            slots.append(permute(far, "dp", lambda i: i ^ 1))
        else:
            slots.append(permute(v, "dp", lambda i: ((i + 2 * k) % n) ^ 1))
    return slots


def after(v, *deps):
    return lax.optimization_barrier((v,) + deps)[0]


def dp_slots():
    n = lax.axis_size("dp")
    me = lax.axis_index("dp")
    s = jnp.arange(n)
    hops = (me // 2 - s // 2) % (n // 2)
    return (2 * hops + ((s ^ me) & 1)).astype(jnp.int32)


def row(v):
    return v.reshape(1, -1)


def per_device(
    features,
    position,
    image_sizes,
    gain_early,
    bias_early,
    conv_early,
    conv_bias_early,
    down_early,
    down_bias_early,
    up_early,
    up_bias_early,
    gain_late,
    bias_late,
    conv_late,
    conv_bias_late,
    down_late,
    down_bias_late,
    up_late,
    up_bias_late,
    readout_in,
    readout_in_bias,
    readout_out,
    readout_out_bias,
    out_grad,
):
    mp = lax.axis_size("mp")
    dp = lax.axis_size("dp")
    width = features.shape[0]
    channels = width * mp
    n = SIDE * SIDE
    n2 = GRID * GRID
    se = down_early.shape[1]
    cols = readout_in.shape[1]
    out_cols = readout_out.shape[1]
    half = mp // 2
    slot = dp_slots()
    me = lax.axis_index("mp")
    place = lax.axis_index("dp").reshape(1).astype(jnp.int32)
    mine = me.reshape(1).astype(jnp.int32)
    step = jnp.arange(half)
    sides = (me % 2) ^ jnp.arange(2)[:, None]
    send_order = (((me // 2 + step) % half)[None] * 2 + sides).reshape(-1).astype(jnp.int32)
    got_order = (((me // 2 - step) % half)[None] * 2 + sides).reshape(-1).astype(jnp.int32)

    feats = jnp.transpose(features.reshape(width, n))
    posn = jnp.transpose(position)
    w_early = jnp.transpose(conv_early, (1, 0, 2))
    w_late = jnp.transpose(conv_late, (1, 0, 2))
    pool = jnp.where(
        image_sizes[0] == SIDE, pool_matrix(SIDE, SIDE, GRID), pool_matrix(SMALL, SIDE, GRID)
    )
    pp = (pool[:, None, :, None] * pool[None, :, None, :]).reshape(n2, n).astype(BF16)
    vecs = (gain_early, bias_early, gain_late, bias_late, up_bias_early, up_bias_late)
    part = se // dp
    up_at = n + lead_rows(n, width)
    tall = up_at + 2 * part
    (pay,) = call(
        prep_kernel, (shape((mp, tall, width), BF16),), place, image_sizes, feats, posn,
        up_early, up_late, *[row(v) for v in vecs], smem=(0, 1), name="prep",
    )
    x_all = swap(pay)

    gact = pl.pallas_call(
        act_grad_kernel,
        out_shape=shape((mp, n2, cols), BF16),
        grid_spec=pltpu.PrefetchScalarGridSpec(
            num_scalar_prefetch=1,
            grid=(mp,),
            in_specs=[
                pl.BlockSpec((n2, out_cols), lambda j, o: (0, 0)),
                pl.BlockSpec((cols, out_cols), lambda j, o: (o[j], 0)),
            ],
            out_specs=pl.BlockSpec((1, n2, cols), lambda j, o: (j, 0, 0)),
        ),
        cost_estimate=cost(2 * n2 * out_cols * cols * mp, cols * mp * out_cols * 2),
        name="act_grad",
    )(send_order, out_grad, readout_out)
    theirs = permute(gact[half:], "mp", lambda i: i ^ 1)
    x_all = after(x_all, gact)
    gact = (gact[:half].astype(F32) + theirs.astype(F32)).astype(BF16)
    gact = [gact[0]] + [permute(gact[k], "mp", lambda i: i + 2 * k) for k in range(1, half)]

    up1_all, up2_all = unpack_up(slot, dp_gather(x_all[:, up_at:]), se, channels)
    tail0 = -(-(se // width) // 8) * 8
    tail1 = tail_rows(3 * (se // width))
    tail2 = tail_rows(3 * (se // width) + 6)
    vec_all, hid, pay, pool_a, pool_b, sq1 = call(
        front_kernel,
        (
            shape((8, channels)), shape((n, channels), BF16), shape((mp, n2 + tail0, width)),
            shape((n2, channels)), shape((n2, width)), shape((1, width)),
        ),
        image_sizes, x_all, w_early, row(conv_bias_early), pp, down_early,
        smem=(0,), flops=2 * n * channels * 9 * width, name="front",
    )
    b_all = swap(pay)
    normed1, inv1, slope1 = call(
        early_slope_kernel,
        (shape((n, channels)), shape((n, 128)), shape((n, channels))),
        image_sizes, x_all, vec_all, smem=(0,), name="early_slope",
    )
    hids = dp_gather(hid)
    b_all = after(b_all, slope1)
    hid2, pooled, pay, conv2, sq2, rpre1, e1, e1_all = call(
        late_kernel,
        (
            shape((n2, channels), BF16), shape((n2, channels)), shape((mp, n2 + tail0, width)),
            shape((n2, width)), shape((1, width)), shape((1, se)), shape((1, width)),
            shape((1, channels)),
        ),
        b_all, pool_a, up1_all, row(down_bias_early), vec_all, up_early, row(up_bias_early),
        w_late, row(conv_bias_late), down_late,
        flops=2 * n2 * channels * 9 * width, name="late",
    )
    c_all = swap(pay)
    normed2, inv2, slope2 = call(
        late_slope_kernel,
        (shape((n2, channels)), shape((n2, 128)), shape((n2, channels))),
        pooled, vec_all, name="late_slope",
    )
    c_all = after(c_all, slope2)
    tok, act, gpre, pay, rpre2, e2, _ = call(
        readout_kernel,
        (
            shape((n2, channels), BF16), shape((n2, cols), BF16), shape((n2, cols), BF16),
            shape((mp, n2 + tail1, width), BF16), shape((1, se)), shape((1, width)),
            shape((1, channels)),
        ),
        c_all, pooled, up2_all, row(down_bias_late), vec_all, up_late, row(up_bias_late),
        readout_in, row(readout_in_bias), *gact,
        flops=4 * n2 * channels * cols, name="readout",
    )
    gtok = swap(pay)
    cats = dp_gather(jnp.concatenate([tok, hid2, gpre, out_grad], axis=1))
    act0 = jnp.stack([act] + [permute(act, "mp", lambda i: i + 2 * k) for k in range(1, half)])
    act1 = permute(act0, "mp", lambda i: i ^ 1)
    tokens_out = pl.pallas_call(
        logits_kernel,
        out_shape=shape((n2, out_cols), BF16),
        grid_spec=pltpu.PrefetchScalarGridSpec(
            num_scalar_prefetch=1,
            grid=(mp,),
            in_specs=[
                pl.BlockSpec((1, n2, cols), lambda j, o: (jnp.minimum(j, half - 1), 0, 0)),
                pl.BlockSpec((1, n2, cols), lambda j, o: (jnp.maximum(j - half, 0), 0, 0)),
                pl.BlockSpec((cols, out_cols), lambda j, o: (o[j], 0)),
                pl.BlockSpec((1, out_cols), lambda j, o: (0, 0)),
            ],
            out_specs=pl.BlockSpec((n2, out_cols), lambda j, o: (0, 0)),
            scratch_shapes=[pltpu.VMEM((n2, out_cols), F32)],
        ),
        cost_estimate=cost(2 * n2 * out_cols * cols * mp, cols * mp * out_cols * 2),
        name="logits",
    )(got_order, act0, act1, readout_out, row(readout_out_bias))

    gconv2, grp2, gl2, pay = call(
        late_back_kernel,
        (
            shape((n2, width), BF16), shape((1, se)), shape((1, width)),
            shape((mp, n2 + tail2, width), BF16),
        ),
        mine, gtok, conv2, e2, rpre2, down_late, w_late, normed2, inv2, slope2, vec_all,
        b_all, e1_all, up1_all,
        smem=(0,), flops=2 * n2 * channels * 9 * width, name="late_back",
    )
    part2 = after(swap(pay), tokens_out)
    gae, gconv1, grp1, gl1, gg2, pay = call(
        early_back_kernel,
        (
            shape((n, width)), shape((n, width), BF16), shape((1, se)), shape((1, width)),
            shape((2, width)), shape((mp, n + 16, width), BF16),
        ),
        image_sizes, part2, pool_b, e1, rpre1, down_early, pp, w_early, normed1, inv1, slope1, vec_all,
        smem=(0,), flops=2 * n * channels * 9 * width, name="early_back",
    )
    part1 = swap(pay)
    (parcel,) = call(
        parcel_kernel, (shape((n + n2 + tail_rows(12 * (se // width) + 18), width), BF16),),
        gconv1, gconv2, rpre1, rpre2, grp1, grp2, gl1, gl2, sq1, sq2, gg2, name="parcel",
    )
    parcels = dp_gather(parcel, relay=False)
    grad_w2, grad_cb2, grad_in_w, grad_in_b = late_weights(slot, cats, parcels, channels, cols, 2)
    grad_w1, grad_cb1 = early_weights(slot, hids, parcels, 2)
    grad_down1, grad_up1, grad_down2, grad_up2, flat, lines = small_grads(slot, parcels, se)
    part1 = after(part1, grad_w1, grad_w2, flat)
    fgrad, low = call(
        final_kernel, (shape((n, width)), shape((n + 16, width), BF16)),
        image_sizes, part1, gae, smem=(0,), name="final",
    )
    pos_grad, gg1 = position_sum(slot, dp_gather(low, relay=False))
    grad_out_w, grad_out_b = act_weights(
        slot, got_order, dp_gather(act0), dp_gather(act1), cats, 2 * channels + cols, out_cols
    )

    return (
        tokens_out,
        jnp.transpose(fgrad).reshape(width, 1, n),
        jnp.transpose(pos_grad),
        gg1[0],
        gg1[1],
        jnp.transpose(grad_w1, (1, 0, 2)),
        grad_cb1[0],
        grad_down1,
        flat[0],
        grad_up1,
        lines[0],
        lines[2],
        lines[3],
        jnp.transpose(grad_w2, (1, 0, 2)),
        grad_cb2[0],
        grad_down2,
        flat[1],
        grad_up2,
        lines[1],
        grad_in_w,
        grad_in_b[0],
        grad_out_w,
        grad_out_b[0],
    )


def solution(mesh):
    by_mp = P("mp")
    block = (by_mp, by_mp, P(None, None, "mp"), by_mp, P("mp", None), P(), P(None, "mp"), by_mp)
    return jax.shard_map(
        per_device,
        mesh=mesh,
        in_specs=(P("mp", "dp", None), P("mp", None), P("dp"))
        + block
        + block
        + (P(None, "mp"), by_mp, P(None, "mp"), by_mp, P("dp", "mp")),
        out_specs=(P("dp", "mp"), P("mp", "dp", None), P("mp", None))
        + block
        + block
        + (P(None, "mp"), by_mp, P(None, "mp"), by_mp),
        check_vma=False,
    )
```

```python
from functools import partial

import jax
import jax.numpy as jnp
from jax import lax
from jax.experimental import pallas as pl
from jax.experimental.pallas import tpu as pltpu
from jax.sharding import PartitionSpec as P

SIDE = 24
SMALL = 16
GRID = 12
EPS = 1e-06
F32 = jnp.float32
BF16 = jnp.bfloat16
HI = lax.Precision.HIGHEST


def pool_matrix(extent, side_len, grid_len):
    row_index = jnp.arange(grid_len)[:, None]
    col_index = jnp.arange(side_len)[None, :]
    first_col = row_index * extent // grid_len
    end_col = -(-(row_index + 1) * extent // grid_len)
    in_bin = (col_index >= first_col) & (col_index < end_col)
    return jnp.where(in_bin, 1.0, 0.0).astype(F32) / (end_col - first_col).astype(F32)


def shape(dims, dtype=F32):
    return jax.ShapeDtypeStruct(dims, dtype)


def cost(flops, nbytes):
    return pl.CostEstimate(flops=int(flops), bytes_accessed=int(nbytes), transcendentals=0)


def call(kernel, outs, *args, flops=1e6, smem=(), name=None):
    specs = [
        pl.BlockSpec(memory_space=pltpu.SMEM if k in smem else pltpu.VMEM)
        for k in range(len(args))
    ]
    nbytes = sum(a.size * a.dtype.itemsize for a in args) + sum(
        o.size * jnp.dtype(o.dtype).itemsize for o in outs
    )
    return pl.pallas_call(
        kernel,
        out_shape=list(outs),
        in_specs=specs,
        out_specs=[pl.BlockSpec(memory_space=pltpu.VMEM) for _ in outs],
        cost_estimate=cost(flops, nbytes),
        name=name,
    )(*args)


def mm(a, b, ca, cb, precision=None):
    return lax.dot_general(
        a, b, (((ca,), (cb,)), ((), ())), preferred_element_type=F32, precision=precision
    )


def sigmoid(v):
    return 1.0 / (1.0 + jnp.exp(-v))


def silu_grad(v):
    s = sigmoid(v)
    return s * (1.0 + v * (1.0 - s))


def grid_rc(side, lanes):
    i = lax.broadcasted_iota(jnp.int32, (side * side, lanes), 0).astype(F32)
    r = jnp.floor((i + 0.5) * (1.0 / side))
    return r, i - r * side


def tap_ok(r, c, side, dy, dx):
    ok = None
    for v, d in ((r, dy), (c, dx)):
        if d == 0:
            continue
        one = (v >= 0.5) if d < 0 else (v <= side - 1.5)
        ok = one if ok is None else ok & one
    return ok


def tap_sum(y, side, width):
    n = side * side
    r, c = grid_rc(side, width)
    total = None
    for t in range(9):
        dy, dx = t // 3 - 1, t % 3 - 1
        part = y[:, t * width : (t + 1) * width]
        off = dy * side + dx
        if off:
            part = pltpu.roll(part, (-off) % n, 0)
        ok = tap_ok(r, c, side, dy, dx)
        if ok is not None:
            part = jnp.where(ok, part, 0.0)
        total = part if total is None else total + part
    return total


def tap_spread(g, side, width):
    n = side * side
    r, c = grid_rc(side, width)
    parts = []
    for t in range(9):
        dy, dx = t // 3 - 1, t % 3 - 1
        off = dy * side + dx
        part = pltpu.roll(g, off % n, 0) if off else g
        ok = tap_ok(r, c, side, -dy, -dx)
        if ok is not None:
            part = jnp.where(ok, part, 0.0)
        parts.append(part.astype(BF16))
    return jnp.concatenate(parts, axis=1)


def wide(ref):
    return jnp.concatenate([ref[j] for j in range(ref.shape[0])], axis=1)


def split_mm(p, v, ca, cb):
    top = v.astype(BF16)
    low = (v - top.astype(F32)).astype(BF16)
    return mm(p, top, ca, cb) + mm(p, low, ca, cb)


def size_mask(size, width):
    r, c = grid_rc(SIDE, width)
    s = size.astype(F32) - 0.5
    return jnp.where((r < s) & (c < s), 1.0, 0.0).astype(F32)


def put_all(ref, value):
    for j in range(ref.shape[0]):
        ref[j] = value


def pieces_of(v, count):
    out = []
    for _ in range(count):
        top = v.astype(BF16).astype(F32)
        out.append(top)
        v = v - top
    return out


def tail_rows(total):
    return -(-total // 16) * 16


def pack(rows, width):
    height = tail_rows(len(rows))
    index = lax.broadcasted_iota(jnp.int32, (height, width), 0)
    out = jnp.zeros((height, width), F32)
    for k, one in enumerate(rows):
        out = jnp.where(index == k, one, out)
    return out.astype(BF16)


def chop(v, width):
    return [
        p[:, k * width : (k + 1) * width]
        for p in pieces_of(v, 3)
        for k in range(v.shape[1] // width)
    ]


def join(acc, first, length):
    k = length // acc.shape[1]
    rows = [acc[first + i : first + i + 1] for i in range(3 * k)]
    return jnp.concatenate([rows[i] + rows[k + i] + rows[2 * k + i] for i in range(k)], axis=1)


def plain_join(acc, length):
    k = length // acc.shape[1]
    return jnp.concatenate([acc[i : i + 1] for i in range(k)], axis=1)


def block_sum(ref, first, last):
    acc = ref[0, first:last, :].astype(F32)
    for j in range(1, ref.shape[0]):
        acc = acc + ref[j, first:last, :].astype(F32)
    return acc


def wide_rows(ref, first, last):
    return jnp.concatenate([ref[j, first:last, :] for j in range(ref.shape[0])], axis=1)


def two_mm(v, w, cb):
    top, low = pieces_of(jnp.broadcast_to(v, (8, v.shape[1])), 2)
    return (mm(top.astype(BF16), w, 1, cb) + mm(low.astype(BF16), w, 1, cb))[0:1]


def small_mm(v, w, cb):
    return mm(jnp.broadcast_to(v, (8, v.shape[1])), w, 1, cb, HI)[0:1]


def per_side(size, width):
    size = size.astype(F32)
    return 1.0 / (size * size + jnp.zeros((1, width), F32))


def silu(v):
    return v * sigmoid(v)


def flat_rows(v, width):
    return [v[:, k * width : (k + 1) * width] for k in range(v.shape[1] // width)]


def pack32(rows, width):
    height = -(-len(rows) // 8) * 8
    index = lax.broadcasted_iota(jnp.int32, (height, width), 0)
    out = jnp.zeros((height, width), F32)
    for k, one in enumerate(rows):
        out = jnp.where(index == k, one, out)
    return out


def lead_rows(n, width):
    return tail_rows(12 + -(-n // width))


def prep_kernel(place_ref, size_ref, f_ref, p_ref, up1_ref, up2_ref, *rest):
    vec_refs, out_ref = rest[:-1], rest[-1]
    n, width = f_ref.shape
    x = (f_ref[...].astype(F32) + p_ref[...].astype(F32)) * size_mask(size_ref[0], width)
    middle = (jnp.sum(x, axis=1, keepdims=True) * (1.0 / width)).astype(BF16).astype(F32)
    lane = lax.broadcasted_iota(jnp.int32, (n, width), 1)
    line = mm(jnp.ones((8, width), F32), jnp.where(lane == 0, middle, 0.0), 1, 1)[0:1]
    count = -(-n // width)
    if count * width > n:
        line = jnp.concatenate([line, jnp.zeros((1, count * width - n), F32)], axis=1)
    rows = []
    for ref in vec_refs:
        rows += pieces_of(ref[...], 2)
    rows += flat_rows(line, width)
    part = (out_ref.shape[1] - n - tail_rows(len(rows))) // 2
    start = pl.multiple_of(place_ref[0] * part, part)
    up = [r[pl.ds(start, part), :].astype(BF16) for r in (up1_ref, up2_ref)]
    value = jnp.concatenate([(x - middle).astype(BF16), pack(rows, width)] + up, axis=0)
    put_all(out_ref, value)


def lead_of(x_ref, n):
    width = x_ref.shape[2]
    return [x_ref[j, n : n + lead_rows(n, width), :].astype(F32) for j in range(x_ref.shape[0])]


def restore_x(x_ref, lead, n):
    blocks, _, width = x_ref.shape
    count = -(-n // width)
    lines = [
        jnp.concatenate([p[12 + k : 13 + k] for k in range(count)], axis=1)[:, :n] for p in lead
    ]
    lines = jnp.concatenate(lines, axis=0)
    shape2 = (blocks, blocks * width)
    col = lax.broadcasted_iota(jnp.int32, shape2, 1).astype(F32)
    home = lax.broadcasted_iota(jnp.int32, shape2, 0).astype(F32)
    here = jnp.floor((col + 0.5) * (1.0 / width)) == home
    spread = mm(lines, jnp.where(here, 1.0, 0.0).astype(F32), 0, 0)
    return wide_rows(x_ref, 0, n).astype(F32) + spread


def unpack_up_kernel(images, slot_ref, *refs):
    parts, (up1_ref, up2_ref, buf_ref, sems) = refs[:images], refs[images:]
    fetch(slot_ref, parts, buf_ref, sems, whole_ref)
    arrive(parts, buf_ref, sems, whole_ref)
    q = buf_ref.shape[2] // 2
    for s in range(images):
        both = jnp.concatenate([buf_ref[s, j] for j in range(buf_ref.shape[1])], axis=1)
        up1_ref[s * q : (s + 1) * q, :] = both[:q]
        up2_ref[s * q : (s + 1) * q, :] = both[q:]


def unpack_up(slot, parts, se, channels):
    images = len(parts)
    return pl.pallas_call(
        partial(unpack_up_kernel, images),
        out_shape=[shape((se, channels), BF16), shape((se, channels), BF16)],
        in_specs=[pl.BlockSpec(memory_space=pltpu.SMEM)] + any_specs(images),
        out_specs=[pl.BlockSpec(memory_space=pltpu.VMEM)] * 2,
        scratch_shapes=[
            pltpu.VMEM((images,) + parts[0].shape, BF16), pltpu.SemaphoreType.DMA((images,))
        ],
        cost_estimate=cost(1e6, 2e6),
        name="unpack_up",
    )(slot, *parts)


def norm_rows(x, gain, bias):
    scale = 1.0 / x.shape[1]
    center = jnp.sum(x, axis=1, keepdims=True) * scale
    d = x - center
    inv = lax.rsqrt(jnp.sum(d * d, axis=1, keepdims=True) * scale + EPS)
    normed = d * inv
    return normed, inv, normed * gain + bias


def front_kernel(
    size_ref, x_ref, w_ref, cb_ref, pp_ref, down_ref, vec_ref, h_ref, pay_ref, a_ref, b_ref, sq_ref
):
    out = w_ref.shape[2]
    blocks = x_ref.shape[0]
    n = SIDE * SIDE
    packed = lead_of(x_ref, n)
    x = restore_x(x_ref, packed, n)
    a_ref[...] = split_mm(pp_ref[...], x, 1, 0)
    for k in range(6):
        vec_ref[k : k + 1] = jnp.concatenate(
            [p[2 * k : 2 * k + 1] + p[2 * k + 1 : 2 * k + 2] for p in packed], axis=1
        )
    vec_ref[6:8] = jnp.zeros((2, vec_ref.shape[1]), F32)
    _, _, pre = norm_rows(x, vec_ref[0:1], vec_ref[1:2])
    mask = size_mask(size_ref[0], out)
    h = (silu(pre) * jnp.concatenate([mask] * blocks, axis=1)).astype(BF16)
    h_ref[...] = h
    y = mm(h, wide(w_ref), 1, 0)
    conv = (tap_sum(y, SIDE, out) + cb_ref[...]) * mask
    pooled = split_mm(pp_ref[...], conv, 1, 0)
    b_ref[...] = pooled
    sq = jnp.sum(conv, axis=0, keepdims=True) * per_side(size_ref[0], out)
    sq_ref[...] = sq
    tail = pack32(flat_rows(small_mm(sq, down_ref[...], 0), out), out)
    put_all(pay_ref, jnp.concatenate([pooled, tail], axis=0))


def early_slope_kernel(size_ref, x_ref, vec_ref, n_ref, i_ref, d_ref):
    blocks, _, width = x_ref.shape
    x = restore_x(x_ref, lead_of(x_ref, SIDE * SIDE), SIDE * SIDE)
    normed, inv, pre = norm_rows(x, vec_ref[0:1], vec_ref[1:2])
    n_ref[...] = normed
    i_ref[...] = jnp.broadcast_to(inv, i_ref.shape)
    mask = size_mask(size_ref[0], width)
    d_ref[...] = silu_grad(pre) * jnp.concatenate([mask] * blocks, axis=1)


def late_kernel(
    ball_ref, a_ref, up_all_ref, db_ref, vec_ref, up_ref, ub_ref, w_ref, cb_ref, down_ref,
    h_ref, pool_ref, pay_ref, conv_ref, sq_ref, rpre_ref, e_ref, eall_ref,
):
    out = w_ref.shape[2]
    n = GRID * GRID
    rpre = plain_join(block_sum(ball_ref, n, ball_ref.shape[1]), db_ref.shape[1]) + db_ref[...]
    rpre_ref[...] = rpre
    red = silu(rpre)
    e_all = sigmoid(two_mm(red, up_all_ref[...], 0) + vec_ref[4:5])
    eall_ref[...] = e_all
    e_ref[...] = sigmoid(small_mm(red, up_ref[...], 0) + ub_ref[...])
    pooled = a_ref[...] + wide_rows(ball_ref, 0, n) * e_all
    pool_ref[...] = pooled
    _, _, pre = norm_rows(pooled, vec_ref[2:3], vec_ref[3:4])
    h = silu(pre).astype(BF16)
    h_ref[...] = h
    y = mm(h, wide(w_ref), 1, 0)
    conv = tap_sum(y, GRID, out) + cb_ref[...]
    conv_ref[...] = conv
    sq = jnp.sum(conv, axis=0, keepdims=True) * (1.0 / n)
    sq_ref[...] = sq
    tail = pack32(flat_rows(small_mm(sq, down_ref[...], 0), out), out)
    put_all(pay_ref, jnp.concatenate([conv, tail], axis=0))


def late_slope_kernel(pool_ref, vec_ref, n_ref, i_ref, d_ref):
    normed, inv, pre = norm_rows(pool_ref[...], vec_ref[2:3], vec_ref[3:4])
    n_ref[...] = normed
    i_ref[...] = jnp.broadcast_to(inv, i_ref.shape)
    d_ref[...] = silu_grad(pre)


def put_blocks(ref, values, tails):
    step = ref.shape[2]
    for j in range(ref.shape[0]):
        tail = tails if not isinstance(tails, list) else tails[j]
        block = values[:, j * step : (j + 1) * step].astype(BF16)
        ref[j] = jnp.concatenate([block, tail], axis=0)


def readout_kernel(
    call_ref, pool_ref, up_all_ref, db_ref, vec_ref, up_ref, ub_ref, w_ref, b_ref, *rest
):
    gh_refs = rest[:-7]
    t_ref, act_ref, gp_ref, pay_ref, rpre_ref, e_ref, spare_ref = rest[-7:]
    n = GRID * GRID
    width = pay_ref.shape[2]
    rpre = plain_join(block_sum(call_ref, n, call_ref.shape[1]), db_ref.shape[1]) + db_ref[...]
    rpre_ref[...] = rpre
    red = silu(rpre)
    e_all = sigmoid(two_mm(red, up_all_ref[...], 0) + vec_ref[5:6])
    spare_ref[...] = e_all
    e_ref[...] = sigmoid(small_mm(red, up_ref[...], 0) + ub_ref[...])
    conv = wide_rows(call_ref, 0, n)
    tok = (pool_ref[...] + conv * e_all).astype(BF16)
    t_ref[...] = tok
    pre = mm(tok, w_ref[...], 1, 0) + b_ref[...]
    phi = 0.5 * (1.0 + lax.erf(pre * 0.7071067811865476))
    act_ref[...] = (pre * phi).astype(BF16)
    dens = 0.3989422804014327 * jnp.exp(-0.5 * pre * pre)
    gh = gh_refs[0][...].astype(F32)
    for one in gh_refs[1:]:
        gh = gh + one[...].astype(F32)
    gp = (gh * (phi + pre * dens)).astype(BF16)
    gp_ref[...] = gp
    gt = mm(gp, w_ref[...], 1, 1)
    gl = jnp.sum(gt * conv, axis=0, keepdims=True) * e_all * (1.0 - e_all)
    put_blocks(pay_ref, gt, pack(chop(two_mm(gl, up_all_ref[...], 1), width), width))


def act_grad_kernel(order_ref, g_ref, w_ref, out_ref):
    out_ref[0] = mm(g_ref[...], w_ref[...], 1, 1).astype(BF16)


def logits_kernel(blocks_ref, a0_ref, a1_ref, w_ref, b_ref, out_ref, acc_ref):
    j = pl.program_id(0)
    half = pl.num_programs(0) // 2

    @pl.when(j == 0)
    def _():
        acc_ref[...] = jnp.zeros_like(acc_ref)

    @pl.when(j < half)
    def _():
        acc_ref[...] += mm(a0_ref[0], w_ref[...], 1, 0)

    @pl.when(j >= half)
    def _():
        acc_ref[...] += mm(a1_ref[0], w_ref[...], 1, 0)

    @pl.when(j == pl.num_programs(0) - 1)
    def _():
        out_ref[...] = (acc_ref[...] + b_ref[...]).astype(BF16)


def squeeze_back(gr, rpre_ref, down_ref, grp_ref):
    grp = gr * silu_grad(rpre_ref[...])
    grp_ref[...] = grp
    return small_mm(grp, down_ref[...], 1)


def norm_back(gh, d_ref, n_ref, i_ref, gain):
    normed = n_ref[...]
    gpre = gh * d_ref[...]
    scale = 1.0 / gh.shape[1]
    g_gain = jnp.sum(gpre * normed, axis=0, keepdims=True)
    g_bias = jnp.sum(gpre, axis=0, keepdims=True)
    gn = gpre * gain
    m1 = jnp.sum(gn, axis=1, keepdims=True) * scale
    m2 = jnp.sum(gn * normed, axis=1, keepdims=True) * scale
    return (gn - m1 - normed * m2) * i_ref[:, 0:1], g_gain, g_bias


def gain_tails(extra, g_gain, g_bias, width, blocks):
    tails = []
    for j in range(blocks):
        rows = list(extra)
        for v in (g_gain, g_bias):
            rows += pieces_of(v[:, j * width : (j + 1) * width], 3)
        tails.append(pack(rows, width))
    return tails


def late_back_kernel(
    me_ref, gt_ref, conv_ref, e_ref, rpre_ref, down_ref, w_ref, n_ref, i_ref, d_ref, vec_ref,
    ball_ref, eall_ref, up_all_ref, gc_ref, grp_ref, gl_ref, pay_ref,
):
    out = w_ref.shape[2]
    blocks = pay_ref.shape[0]
    n = GRID * GRID
    se = rpre_ref.shape[1]
    g = block_sum(gt_ref, 0, n)
    e = e_ref[...]
    gl_ref[...] = jnp.sum(g * conv_ref[...], axis=0, keepdims=True) * e * (1.0 - e)
    gr = join(block_sum(gt_ref, n, gt_ref.shape[1]), 0, se)
    gs = squeeze_back(gr, rpre_ref, down_ref, grp_ref)
    gc = (g * e + gs * (1.0 / n)).astype(BF16)
    gc_ref[...] = gc
    gh = mm(tap_spread(gc.astype(F32), GRID, out), wide(w_ref), 1, 1)
    part, g_gain, g_bias = norm_back(gh, d_ref, n_ref, i_ref, vec_ref[2:3])
    own = [g * jnp.where(me_ref[0] == j, 1.0, 0.0).astype(F32) for j in range(blocks)]
    part = part + jnp.concatenate(own, axis=1)
    e_all = eall_ref[...]
    pooled = wide_rows(ball_ref, 0, n)
    gl1 = jnp.sum(part * pooled, axis=0, keepdims=True) * e_all * (1.0 - e_all)
    extra = chop(two_mm(gl1, up_all_ref[...], 1), out)
    put_blocks(pay_ref, part, gain_tails(extra, g_gain, g_bias, out, blocks))


def early_back_kernel(
    size_ref, p2_ref, b_ref, e_ref, rpre_ref, down_ref, pp_ref, w_ref, n_ref, i_ref, d_ref, vec_ref,
    gae_ref, gc_ref, grp_ref, gl_ref, gg_ref, pay_ref,
):
    out = w_ref.shape[2]
    blocks = pay_ref.shape[0]
    n2 = GRID * GRID
    se = rpre_ref.shape[1]
    g = block_sum(p2_ref, 0, n2)
    tail = block_sum(p2_ref, n2, p2_ref.shape[1])
    e = e_ref[...]
    gl_ref[...] = jnp.sum(g * b_ref[...], axis=0, keepdims=True) * e * (1.0 - e)
    used = 3 * (se // out)
    gg_ref[0:1] = join(tail, used, out)
    gg_ref[1:2] = join(tail, used + 3, out)
    gs = squeeze_back(join(tail, 0, se), rpre_ref, down_ref, grp_ref) * per_side(size_ref[0], out)
    gae = split_mm(pp_ref[...], g, 0, 0)
    gae_ref[...] = gae
    gc = ((gae * e + gs) * size_mask(size_ref[0], out)).astype(BF16)
    gc_ref[...] = gc
    gh = mm(tap_spread(gc.astype(F32), SIDE, out), wide(w_ref), 1, 1)
    part, g_gain, g_bias = norm_back(gh, d_ref, n_ref, i_ref, vec_ref[0:1])
    put_blocks(pay_ref, part, gain_tails([], g_gain, g_bias, out, blocks))


def final_kernel(size_ref, p1_ref, gae_ref, fg_ref, low_ref):
    n, width = gae_ref.shape
    out = (gae_ref[...] + block_sum(p1_ref, 0, n)) * size_mask(size_ref[0], width)
    fg_ref[...] = out
    tail = block_sum(p1_ref, n, p1_ref.shape[1])
    rows = []
    for k in range(2):
        rows += pieces_of(join(tail, 3 * k, width), 3)
    low_ref[...] = jnp.concatenate([out.astype(BF16), pack(rows, width)], axis=0)


def fetch(slot_ref, refs, dst_ref, sems, pick):
    for s in range(len(refs)):
        for q, ref in enumerate(refs):

            @pl.when(slot_ref[s] == q)
            def _():
                pltpu.make_async_copy(pick(ref), dst_ref.at[s], sems.at[s]).start()


def arrive(refs, dst_ref, sems, pick):
    for s in range(len(refs)):
        pltpu.make_async_copy(pick(refs[0]), dst_ref.at[s], sems.at[s]).wait()


def any_specs(count):
    return [pl.BlockSpec(memory_space=pl.ANY)] * count


def whole_ref(ref):
    return ref


def position_kernel(images, slot_ref, *refs):
    lows, (pos_ref, gg_ref, buf_ref, sems) = refs[:images], refs[images:]
    fetch(slot_ref, lows, buf_ref, sems, whole_ref)
    arrive(lows, buf_ref, sems, whole_ref)
    n = pos_ref.shape[0]
    acc = buf_ref[0].astype(F32)
    for s in range(1, images):
        acc = acc + buf_ref[s].astype(F32)
    pos_ref[...] = acc[:n]
    for k in range(2):
        gg_ref[k : k + 1] = join(acc[n:], 3 * k, acc.shape[1])


def position_sum(slot, lows):
    images = len(lows)
    tall, width = lows[0].shape
    n = SIDE * SIDE
    return pl.pallas_call(
        partial(position_kernel, images),
        out_shape=[shape((n, width)), shape((2, width))],
        in_specs=[pl.BlockSpec(memory_space=pltpu.SMEM)] + any_specs(images),
        out_specs=[pl.BlockSpec(memory_space=pltpu.VMEM)] * 2,
        scratch_shapes=[
            pltpu.VMEM((images, tall, width), BF16), pltpu.SemaphoreType.DMA((images,))
        ],
        cost_estimate=cost(1e6, images * tall * width * 2),
        name="position",
    )(slot, *lows)


def parcel_kernel(g1_ref, g2_ref, *refs):
    vecs, out_ref = refs[:-1], refs[-1]
    width = out_ref.shape[1]
    rows = []
    for ref in vecs[:2]:
        rows += chop(silu(ref[...]), width)
    for ref in vecs[2:8]:
        rows += chop(ref[...], width)
    rows += chop(vecs[8][0:1], width) + chop(vecs[8][1:2], width)
    out_ref[...] = jnp.concatenate([g1_ref[...], g2_ref[...], pack(rows, width)], axis=0)


def small_kernel(images, se, slot_ref, *refs):
    parcels = refs[:images]
    d1_ref, u1_ref, d2_ref, u2_ref, flat_ref, wide_ref, buf_ref, sems = refs[images:]
    first = SIDE * SIDE + GRID * GRID
    count = buf_ref.shape[1]

    def pick(ref):
        return ref.at[pl.ds(first, count), :]

    fetch(slot_ref, parcels, buf_ref, sems, pick)
    arrive(parcels, buf_ref, sems, pick)
    width = buf_ref.shape[2]
    lengths = [se] * 4 + [width] * 6
    tables = []
    at = 0
    tails = [buf_ref[s].astype(F32) for s in range(images)]
    for length in lengths:
        index = lax.broadcasted_iota(jnp.int32, (8, length), 0)
        table = jnp.zeros((8, length), F32)
        for s in range(images):
            table = jnp.where(index == s, join(tails[s], at, length), table)
        tables.append(table)
        at += 3 * (length // width)
    u1_ref[...] = mm(tables[0], tables[4], 0, 0, HI)
    u2_ref[...] = mm(tables[1], tables[5], 0, 0, HI)
    d1_ref[...] = mm(tables[6], tables[2], 0, 0, HI)
    d2_ref[...] = mm(tables[7], tables[3], 0, 0, HI)
    for k, table in enumerate(tables[2:4]):
        flat_ref[k : k + 1] = jnp.sum(table, axis=0, keepdims=True)
    for k, t in enumerate((4, 5, 8, 9)):
        wide_ref[k : k + 1] = jnp.sum(tables[t], axis=0, keepdims=True)


def small_grads(slot, parcels, se):
    images = len(parcels)
    tall, width = parcels[0].shape
    outs = [(width, se), (se, width), (width, se), (se, width), (2, se), (4, width)]
    return pl.pallas_call(
        partial(small_kernel, images, se),
        out_shape=[shape(o) for o in outs],
        in_specs=[pl.BlockSpec(memory_space=pltpu.SMEM)] + any_specs(images),
        out_specs=[pl.BlockSpec(memory_space=pltpu.VMEM)] * 6,
        scratch_shapes=[
            pltpu.VMEM((images, tall - SIDE * SIDE - GRID * GRID, width), BF16),
            pltpu.SemaphoreType.DMA((images,)),
        ],
        cost_estimate=cost(1e6, 1e6),
        name="small_grads",
    )(slot, *parcels)


def spread_all(images, side, g_ref, spread_ref, gb_ref):
    n = side * side
    total = None
    for s in range(images):
        g = g_ref[s].astype(F32)
        one = jnp.sum(g, axis=0, keepdims=True)
        total = one if total is None else total + one
        spread_ref[s * n : (s + 1) * n, :] = tap_spread(g, side, g.shape[1])
    gb_ref[...] = total


def early_weight_kernel(images, slot_ref, *refs):
    hids, parcels = refs[:images], refs[images : 2 * images]
    out_ref, gb_ref, h_ref, g_ref, spread_ref, sems, sems2 = refs[2 * images :]
    n = SIDE * SIDE
    out = g_ref.shape[2]
    step = pl.program_id(0)
    width = out_ref.shape[1]

    def pick(ref):
        return ref.at[pl.ds(0, n), :]

    @pl.when(step == 0)
    def _():
        fetch(slot_ref, parcels, g_ref, sems2, pick)
        fetch(slot_ref, hids, h_ref, sems, whole_ref)
        arrive(parcels, g_ref, sems2, pick)
        spread_all(images, SIDE, g_ref, spread_ref, gb_ref)
        arrive(hids, h_ref, sems, whole_ref)

    lanes = pl.ds(pl.multiple_of(step * width, width), width)
    h = jnp.concatenate([h_ref[s, :, lanes] for s in range(images)], axis=0)
    res = mm(h, spread_ref[...], 0, 0)
    for t in range(9):
        out_ref[t] = res[:, t * out : (t + 1) * out]


def early_weights(slot, hids, parcels, steps):
    images = len(hids)
    n, channels = hids[0].shape
    out = parcels[0].shape[1]
    rows = channels // steps
    return pl.pallas_call(
        partial(early_weight_kernel, images),
        out_shape=[shape((9, channels, out)), shape((1, out))],
        grid_spec=pltpu.PrefetchScalarGridSpec(
            num_scalar_prefetch=1,
            grid=(steps,),
            in_specs=any_specs(2 * images),
            out_specs=[
                pl.BlockSpec((9, rows, out), lambda k, s: (0, k, 0)),
                pl.BlockSpec((1, out), lambda k, s: (0, 0)),
            ],
            scratch_shapes=[
                pltpu.VMEM((images, n, channels), BF16),
                pltpu.VMEM((images, n, out), BF16),
                pltpu.VMEM((images * n, 9 * out), BF16),
                pltpu.SemaphoreType.DMA((images,)),
                pltpu.SemaphoreType.DMA((images,)),
            ],
        ),
        cost_estimate=cost(
            2 * images * n * 9 * out * channels, images * n * channels * 2 + 36 * channels * out
        ),
        name="early_weights",
    )(slot, *hids, *parcels)


def late_weight_kernel(images, channels, cols, slot_ref, *refs):
    cats, parcels = refs[:images], refs[images : 2 * images]
    w_ref, gb_ref, in_ref, ib_ref, c_ref, g_ref, spread_ref, sems, sems2 = refs[2 * images :]
    n = GRID * GRID
    out = g_ref.shape[2]
    step = pl.program_id(0)
    width = w_ref.shape[1]

    def pick_cat(ref):
        return ref.at[:, pl.ds(0, c_ref.shape[2])]

    def pick(ref):
        return ref.at[pl.ds(SIDE * SIDE, n), :]

    @pl.when(step == 0)
    def _():
        fetch(slot_ref, parcels, g_ref, sems2, pick)
        fetch(slot_ref, cats, c_ref, sems, pick_cat)
        arrive(parcels, g_ref, sems2, pick)
        spread_all(images, GRID, g_ref, spread_ref, gb_ref)
        arrive(cats, c_ref, sems, pick_cat)

    gp = jnp.concatenate([c_ref[s, :, 2 * channels :] for s in range(images)], axis=0)

    @pl.when(step == 0)
    def _():
        ib_ref[...] = jnp.sum(gp.astype(F32), axis=0, keepdims=True)

    lanes = pl.ds(pl.multiple_of(step * width, width), width)
    tok = jnp.concatenate([c_ref[s, :, lanes] for s in range(images)], axis=0)
    in_ref[...] = mm(tok, gp, 0, 0)
    lanes = pl.ds(pl.multiple_of(step * width + channels, width), width)
    h = jnp.concatenate([c_ref[s, :, lanes] for s in range(images)], axis=0)
    res = mm(h, spread_ref[...], 0, 0)
    for t in range(9):
        w_ref[t] = res[:, t * out : (t + 1) * out]


def late_weights(slot, cats, parcels, channels, cols, steps):
    images = len(cats)
    n = cats[0].shape[0]
    out = parcels[0].shape[1]
    rows = channels // steps
    return pl.pallas_call(
        partial(late_weight_kernel, images, channels, cols),
        out_shape=[
            shape((9, channels, out)), shape((1, out)), shape((channels, cols)), shape((1, cols))
        ],
        grid_spec=pltpu.PrefetchScalarGridSpec(
            num_scalar_prefetch=1,
            grid=(steps,),
            in_specs=any_specs(2 * images),
            out_specs=[
                pl.BlockSpec((9, rows, out), lambda k, s: (0, k, 0)),
                pl.BlockSpec((1, out), lambda k, s: (0, 0)),
                pl.BlockSpec((rows, cols), lambda k, s: (k, 0)),
                pl.BlockSpec((1, cols), lambda k, s: (0, 0)),
            ],
            scratch_shapes=[
                pltpu.VMEM((images, n, 2 * channels + cols), BF16),
                pltpu.VMEM((images, n, out), BF16),
                pltpu.VMEM((images * n, 9 * out), BF16),
                pltpu.SemaphoreType.DMA((images,)),
                pltpu.SemaphoreType.DMA((images,)),
            ],
        ),
        cost_estimate=cost(2 * images * n * (9 * out + cols) * channels, 12e6),
        name="late_weights",
    )(slot, *cats, *parcels)


def act_weight_kernel(images, offset, slot_ref, blocks_ref, *refs):
    act0, act1, cats = (refs[k * images : (k + 1) * images] for k in range(3))
    out_ref, gb_ref, a_ref, g_ref, sems0, sems1, sems2 = refs[3 * images :]
    j = pl.program_id(0)
    half = pl.num_programs(0) // 2

    def pick(ref):
        return ref.at[:, pl.ds(offset, g_ref.shape[2])]

    @pl.when(j == 0)
    def _():
        fetch(slot_ref, cats, g_ref, sems2, pick)
        fetch(slot_ref, act0, a_ref.at[0], sems0, whole_ref)
        fetch(slot_ref, act1, a_ref.at[1], sems1, whole_ref)
        arrive(cats, g_ref, sems2, pick)
        arrive(act0, a_ref.at[0], sems0, whole_ref)

    @pl.when(j == half)
    def _():
        arrive(act1, a_ref.at[1], sems1, whole_ref)

    g = jnp.concatenate([g_ref[s] for s in range(images)], axis=0)

    @pl.when(j == 0)
    def _():
        gb_ref[...] = jnp.sum(g.astype(F32), axis=0, keepdims=True)

    side = j // half
    k = j % half
    a = jnp.concatenate([a_ref[side, s, k] for s in range(images)], axis=0)
    out_ref[...] = mm(a, g, 0, 0)


def act_weights(slot, blocks, act0, act1, cats, offset, cols):
    images = len(act0)
    half, rows, width = act0[0].shape
    total = 2 * half
    return pl.pallas_call(
        partial(act_weight_kernel, images, offset),
        out_shape=[shape((total * width, cols)), shape((1, cols))],
        grid_spec=pltpu.PrefetchScalarGridSpec(
            num_scalar_prefetch=2,
            grid=(total,),
            in_specs=any_specs(3 * images),
            out_specs=[
                pl.BlockSpec((width, cols), lambda k, s, b: (b[k], 0)),
                pl.BlockSpec((1, cols), lambda k, s, b: (0, 0)),
            ],
            scratch_shapes=[
                pltpu.VMEM((2, images, half, rows, width), BF16),
                pltpu.VMEM((images, rows, cols), BF16),
            ]
            + [pltpu.SemaphoreType.DMA((images,))] * 3,
        ),
        cost_estimate=cost(
            2 * images * rows * total * width * cols, images * total * rows * width * 2 + total * width * cols * 4
        ),
        name="act_weights",
    )(slot, blocks, *act0, *act1, *cats)


def swap(v):
    return lax.all_to_all(v, "mp", 0, 0)


def permute(v, axis, fn):
    n = lax.axis_size(axis)
    return lax.ppermute(v, axis, [(i, fn(i) % n) for i in range(n)])


def dp_gather(v, relay=True):
    n = lax.axis_size("dp")
    slots = [v, permute(v, "dp", lambda i: i ^ 1)]
    for k in range(1, n // 2):
        far = permute(v, "dp", lambda i: i + 2 * k)
        slots.append(far)
        if relay:
            slots.append(permute(far, "dp", lambda i: i ^ 1))
        else:
            slots.append(permute(v, "dp", lambda i: ((i + 2 * k) % n) ^ 1))
    return slots


def after(v, *deps):
    return lax.optimization_barrier((v,) + deps)[0]


def dp_slots():
    n = lax.axis_size("dp")
    me = lax.axis_index("dp")
    s = jnp.arange(n)
    hops = (me // 2 - s // 2) % (n // 2)
    return (2 * hops + ((s ^ me) & 1)).astype(jnp.int32)


def row(v):
    return v.reshape(1, -1)


def per_device(
    features,
    position,
    image_sizes,
    gain_early,
    bias_early,
    conv_early,
    conv_bias_early,
    down_early,
    down_bias_early,
    up_early,
    up_bias_early,
    gain_late,
    bias_late,
    conv_late,
    conv_bias_late,
    down_late,
    down_bias_late,
    up_late,
    up_bias_late,
    readout_in,
    readout_in_bias,
    readout_out,
    readout_out_bias,
    out_grad,
):
    mp = lax.axis_size("mp")
    dp = lax.axis_size("dp")
    width = features.shape[0]
    channels = width * mp
    n = SIDE * SIDE
    n2 = GRID * GRID
    se = down_early.shape[1]
    cols = readout_in.shape[1]
    out_cols = readout_out.shape[1]
    half = mp // 2
    slot = dp_slots()
    me = lax.axis_index("mp")
    place = lax.axis_index("dp").reshape(1).astype(jnp.int32)
    mine = me.reshape(1).astype(jnp.int32)
    step = jnp.arange(half)
    sides = (me % 2) ^ jnp.arange(2)[:, None]
    send_order = (((me // 2 + step) % half)[None] * 2 + sides).reshape(-1).astype(jnp.int32)
    got_order = (((me // 2 - step) % half)[None] * 2 + sides).reshape(-1).astype(jnp.int32)

    feats = jnp.transpose(features.reshape(width, n))
    posn = jnp.transpose(position)
    w_early = jnp.transpose(conv_early, (1, 0, 2))
    w_late = jnp.transpose(conv_late, (1, 0, 2))
    pool = jnp.where(
        image_sizes[0] == SIDE, pool_matrix(SIDE, SIDE, GRID), pool_matrix(SMALL, SIDE, GRID)
    )
    pp = (pool[:, None, :, None] * pool[None, :, None, :]).reshape(n2, n).astype(BF16)
    vecs = (gain_early, bias_early, gain_late, bias_late, up_bias_early, up_bias_late)
    part = se // dp
    up_at = n + lead_rows(n, width)
    tall = up_at + 2 * part
    (pay,) = call(
        prep_kernel, (shape((mp, tall, width), BF16),), place, image_sizes, feats, posn,
        up_early, up_late, *[row(v) for v in vecs], smem=(0, 1), name="prep",
    )
    x_all = swap(pay)

    gact = pl.pallas_call(
        act_grad_kernel,
        out_shape=shape((mp, n2, cols), BF16),
        grid_spec=pltpu.PrefetchScalarGridSpec(
            num_scalar_prefetch=1,
            grid=(mp,),
            in_specs=[
                pl.BlockSpec((n2, out_cols), lambda j, o: (0, 0)),
                pl.BlockSpec((cols, out_cols), lambda j, o: (o[j], 0)),
            ],
            out_specs=pl.BlockSpec((1, n2, cols), lambda j, o: (j, 0, 0)),
        ),
        cost_estimate=cost(2 * n2 * out_cols * cols * mp, cols * mp * out_cols * 2),
        name="act_grad",
    )(send_order, out_grad, readout_out)
    theirs = permute(gact[half:], "mp", lambda i: i ^ 1)
    gact = (gact[:half].astype(F32) + theirs.astype(F32)).astype(BF16)
    x_all = after(x_all, gact)
    gact = [gact[0]] + [permute(gact[k], "mp", lambda i: i + 2 * k) for k in range(1, half)]

    up1_all, up2_all = unpack_up(slot, dp_gather(x_all[:, up_at:]), se, channels)
    tail0 = -(-(se // width) // 8) * 8
    tail1 = tail_rows(3 * (se // width))
    tail2 = tail_rows(3 * (se // width) + 6)
    vec_all, hid, pay, pool_a, pool_b, sq1 = call(
        front_kernel,
        (
            shape((8, channels)), shape((n, channels), BF16), shape((mp, n2 + tail0, width)),
            shape((n2, channels)), shape((n2, width)), shape((1, width)),
        ),
        image_sizes, x_all, w_early, row(conv_bias_early), pp, down_early,
        smem=(0,), flops=2 * n * channels * 9 * width, name="front",
    )
    b_all = swap(pay)
    normed1, inv1, slope1 = call(
        early_slope_kernel,
        (shape((n, channels)), shape((n, 128)), shape((n, channels))),
        image_sizes, x_all, vec_all, smem=(0,), name="early_slope",
    )
    hids = dp_gather(hid)
    b_all = after(b_all, slope1, *gact[1:])
    hid2, pooled, pay, conv2, sq2, rpre1, e1, e1_all = call(
        late_kernel,
        (
            shape((n2, channels), BF16), shape((n2, channels)), shape((mp, n2 + tail0, width)),
            shape((n2, width)), shape((1, width)), shape((1, se)), shape((1, width)),
            shape((1, channels)),
        ),
        b_all, pool_a, up1_all, row(down_bias_early), vec_all, up_early, row(up_bias_early),
        w_late, row(conv_bias_late), down_late,
        flops=2 * n2 * channels * 9 * width, name="late",
    )
    c_all = swap(pay)
    normed2, inv2, slope2 = call(
        late_slope_kernel,
        (shape((n2, channels)), shape((n2, 128)), shape((n2, channels))),
        pooled, vec_all, name="late_slope",
    )
    c_all = after(c_all, slope2)
    tok, act, gpre, pay, rpre2, e2, _ = call(
        readout_kernel,
        (
            shape((n2, channels), BF16), shape((n2, cols), BF16), shape((n2, cols), BF16),
            shape((mp, n2 + tail1, width), BF16), shape((1, se)), shape((1, width)),
            shape((1, channels)),
        ),
        c_all, pooled, up2_all, row(down_bias_late), vec_all, up_late, row(up_bias_late),
        readout_in, row(readout_in_bias), *gact,
        flops=4 * n2 * channels * cols, name="readout",
    )
    gtok = swap(pay)
    cat = jnp.concatenate([tok, hid2, gpre, out_grad], axis=1)
    cats = dp_gather(cat)
    gtok = after(gtok, cat, *hids[1:3])
    gconv2, grp2, gl2, pay = call(
        late_back_kernel,
        (
            shape((n2, width), BF16), shape((1, se)), shape((1, width)),
            shape((mp, n2 + tail2, width), BF16),
        ),
        mine, gtok, conv2, e2, rpre2, down_late, w_late, normed2, inv2, slope2, vec_all,
        b_all, e1_all, up1_all,
        smem=(0,), flops=2 * n2 * channels * 9 * width, name="late_back",
    )
    acts = [permute(act, "mp", lambda i: i + 2 * k) for k in range(1, half)]
    act0 = jnp.stack([act] + [after(one, grp2) for one in acts])
    act1 = permute(act0, "mp", lambda i: i ^ 1)
    part2 = after(swap(pay), *hids[3:], *cats[1:3])
    gae, gconv1, grp1, gl1, gg2, pay = call(
        early_back_kernel,
        (
            shape((n, width)), shape((n, width), BF16), shape((1, se)), shape((1, width)),
            shape((2, width)), shape((mp, n + 16, width), BF16),
        ),
        image_sizes, part2, pool_b, e1, rpre1, down_early, pp, w_early, normed1, inv1, slope1, vec_all,
        smem=(0,), flops=2 * n * channels * 9 * width, name="early_back",
    )
    part1 = swap(pay)
    (parcel,) = call(
        parcel_kernel, (shape((n + n2 + tail_rows(12 * (se // width) + 18), width), BF16),),
        gconv1, gconv2, rpre1, rpre2, grp1, grp2, gl1, gl2, sq1, sq2, gg2, name="parcel",
    )
    parcels = dp_gather(parcel, relay=False)
    tokens_out = pl.pallas_call(
        logits_kernel,
        out_shape=shape((n2, out_cols), BF16),
        grid_spec=pltpu.PrefetchScalarGridSpec(
            num_scalar_prefetch=1,
            grid=(mp,),
            in_specs=[
                pl.BlockSpec((1, n2, cols), lambda j, o: (jnp.minimum(j, half - 1), 0, 0)),
                pl.BlockSpec((1, n2, cols), lambda j, o: (jnp.maximum(j - half, 0), 0, 0)),
                pl.BlockSpec((cols, out_cols), lambda j, o: (o[j], 0)),
                pl.BlockSpec((1, out_cols), lambda j, o: (0, 0)),
            ],
            out_specs=pl.BlockSpec((n2, out_cols), lambda j, o: (0, 0)),
            scratch_shapes=[pltpu.VMEM((n2, out_cols), F32)],
        ),
        cost_estimate=cost(2 * n2 * out_cols * cols * mp, cols * mp * out_cols * 2),
        name="logits",
    )(got_order, act0, after(act1, parcels[1]), readout_out, row(readout_out_bias))

    grad_w2, grad_cb2, grad_in_w, grad_in_b = late_weights(slot, cats, parcels, channels, cols, 2)
    grad_w1, grad_cb1 = early_weights(slot, hids, parcels, 2)
    grad_down1, grad_up1, grad_down2, grad_up2, flat, lines = small_grads(slot, parcels, se)
    part1 = after(part1, grad_w1, grad_w2, flat, tokens_out)
    fgrad, low = call(
        final_kernel, (shape((n, width)), shape((n + 16, width), BF16)),
        image_sizes, part1, gae, smem=(0,), name="final",
    )
    pos_grad, gg1 = position_sum(slot, dp_gather(low, relay=False))
    grad_out_w, grad_out_b = act_weights(
        slot, got_order, dp_gather(act0), dp_gather(act1), cats, 2 * channels + cols, out_cols
    )

    return (
        tokens_out,
        jnp.transpose(fgrad).reshape(width, 1, n),
        jnp.transpose(pos_grad),
        gg1[0],
        gg1[1],
        jnp.transpose(grad_w1, (1, 0, 2)),
        grad_cb1[0],
        grad_down1,
        flat[0],
        grad_up1,
        lines[0],
        lines[2],
        lines[3],
        jnp.transpose(grad_w2, (1, 0, 2)),
        grad_cb2[0],
        grad_down2,
        flat[1],
        grad_up2,
        lines[1],
        grad_in_w,
        grad_in_b[0],
        grad_out_w,
        grad_out_b[0],
    )


def solution(mesh):
    by_mp = P("mp")
    block = (by_mp, by_mp, P(None, None, "mp"), by_mp, P("mp", None), P(), P(None, "mp"), by_mp)
    return jax.shard_map(
        per_device,
        mesh=mesh,
        in_specs=(P("mp", "dp", None), P("mp", None), P("dp"))
        + block
        + block
        + (P(None, "mp"), by_mp, P(None, "mp"), by_mp, P("dp", "mp")),
        out_specs=(P("dp", "mp"), P("mp", "dp", None), P("mp", None))
        + block
        + block
        + (P(None, "mp"), by_mp, P(None, "mp"), by_mp),
        check_vma=False,
    )
```

```python
from functools import partial

import jax
import jax.numpy as jnp
from jax import lax
from jax.experimental import pallas as pl
from jax.experimental.pallas import tpu as pltpu
from jax.sharding import PartitionSpec as P

SIDE = 24
SMALL = 16
GRID = 12
EPS = 1e-06
F32 = jnp.float32
BF16 = jnp.bfloat16
HI = lax.Precision.HIGHEST


def pool_matrix(extent, side_len, grid_len):
    row_index = jnp.arange(grid_len)[:, None]
    col_index = jnp.arange(side_len)[None, :]
    first_col = row_index * extent // grid_len
    end_col = -(-(row_index + 1) * extent // grid_len)
    in_bin = (col_index >= first_col) & (col_index < end_col)
    return jnp.where(in_bin, 1.0, 0.0).astype(F32) / (end_col - first_col).astype(F32)


def shape(dims, dtype=F32):
    return jax.ShapeDtypeStruct(dims, dtype)


def cost(flops, nbytes):
    return pl.CostEstimate(flops=int(flops), bytes_accessed=int(nbytes), transcendentals=0)


def call(kernel, outs, *args, flops=1e6, smem=(), name=None):
    specs = [
        pl.BlockSpec(memory_space=pltpu.SMEM if k in smem else pltpu.VMEM)
        for k in range(len(args))
    ]
    nbytes = sum(a.size * a.dtype.itemsize for a in args) + sum(
        o.size * jnp.dtype(o.dtype).itemsize for o in outs
    )
    return pl.pallas_call(
        kernel,
        out_shape=list(outs),
        in_specs=specs,
        out_specs=[pl.BlockSpec(memory_space=pltpu.VMEM) for _ in outs],
        cost_estimate=cost(flops, nbytes),
        name=name,
    )(*args)


def mm(a, b, ca, cb, precision=None):
    return lax.dot_general(
        a, b, (((ca,), (cb,)), ((), ())), preferred_element_type=F32, precision=precision
    )


def sigmoid(v):
    return 1.0 / (1.0 + jnp.exp(-v))


def silu_grad(v):
    s = sigmoid(v)
    return s * (1.0 + v * (1.0 - s))


def grid_rc(side, lanes):
    i = lax.broadcasted_iota(jnp.int32, (side * side, lanes), 0).astype(F32)
    r = jnp.floor((i + 0.5) * (1.0 / side))
    return r, i - r * side


def tap_ok(r, c, side, dy, dx):
    ok = None
    for v, d in ((r, dy), (c, dx)):
        if d == 0:
            continue
        one = (v >= 0.5) if d < 0 else (v <= side - 1.5)
        ok = one if ok is None else ok & one
    return ok


def tap_sum(y, side, width):
    n = side * side
    r, c = grid_rc(side, width)
    total = None
    for t in range(9):
        dy, dx = t // 3 - 1, t % 3 - 1
        part = y[:, t * width : (t + 1) * width]
        off = dy * side + dx
        if off:
            part = pltpu.roll(part, (-off) % n, 0)
        ok = tap_ok(r, c, side, dy, dx)
        if ok is not None:
            part = jnp.where(ok, part, 0.0)
        total = part if total is None else total + part
    return total


def tap_spread(g, side, width):
    n = side * side
    r, c = grid_rc(side, width)
    parts = []
    for t in range(9):
        dy, dx = t // 3 - 1, t % 3 - 1
        off = dy * side + dx
        part = pltpu.roll(g, off % n, 0) if off else g
        ok = tap_ok(r, c, side, -dy, -dx)
        if ok is not None:
            part = jnp.where(ok, part, 0.0)
        parts.append(part.astype(BF16))
    return jnp.concatenate(parts, axis=1)


def wide(ref):
    return jnp.concatenate([ref[j] for j in range(ref.shape[0])], axis=1)


def split_mm(p, v, ca, cb):
    top = v.astype(BF16)
    low = (v - top.astype(F32)).astype(BF16)
    return mm(p, top, ca, cb) + mm(p, low, ca, cb)


def size_mask(size, width):
    r, c = grid_rc(SIDE, width)
    s = size.astype(F32) - 0.5
    return jnp.where((r < s) & (c < s), 1.0, 0.0).astype(F32)


def put_all(ref, value):
    for j in range(ref.shape[0]):
        ref[j] = value


def pieces_of(v, count):
    out = []
    for _ in range(count):
        top = v.astype(BF16).astype(F32)
        out.append(top)
        v = v - top
    return out


def tail_rows(total):
    return -(-total // 16) * 16


def pack(rows, width):
    height = tail_rows(len(rows))
    index = lax.broadcasted_iota(jnp.int32, (height, width), 0)
    out = jnp.zeros((height, width), F32)
    for k, one in enumerate(rows):
        out = jnp.where(index == k, one, out)
    return out.astype(BF16)


def chop(v, width):
    return [
        p[:, k * width : (k + 1) * width]
        for p in pieces_of(v, 3)
        for k in range(v.shape[1] // width)
    ]


def join(acc, first, length):
    k = length // acc.shape[1]
    rows = [acc[first + i : first + i + 1] for i in range(3 * k)]
    return jnp.concatenate([rows[i] + rows[k + i] + rows[2 * k + i] for i in range(k)], axis=1)


def plain_join(acc, length):
    k = length // acc.shape[1]
    return jnp.concatenate([acc[i : i + 1] for i in range(k)], axis=1)


def block_sum(ref, first, last):
    acc = ref[0, first:last, :].astype(F32)
    for j in range(1, ref.shape[0]):
        acc = acc + ref[j, first:last, :].astype(F32)
    return acc


def wide_rows(ref, first, last):
    return jnp.concatenate([ref[j, first:last, :] for j in range(ref.shape[0])], axis=1)


def two_mm(v, w, cb):
    top, low = pieces_of(jnp.broadcast_to(v, (8, v.shape[1])), 2)
    return (mm(top.astype(BF16), w, 1, cb) + mm(low.astype(BF16), w, 1, cb))[0:1]


def small_mm(v, w, cb):
    return mm(jnp.broadcast_to(v, (8, v.shape[1])), w, 1, cb, HI)[0:1]


def per_side(size, width):
    size = size.astype(F32)
    return 1.0 / (size * size + jnp.zeros((1, width), F32))


def silu(v):
    return v * sigmoid(v)


def flat_rows(v, width):
    return [v[:, k * width : (k + 1) * width] for k in range(v.shape[1] // width)]


def pack32(rows, width):
    height = -(-len(rows) // 8) * 8
    index = lax.broadcasted_iota(jnp.int32, (height, width), 0)
    out = jnp.zeros((height, width), F32)
    for k, one in enumerate(rows):
        out = jnp.where(index == k, one, out)
    return out


def lead_rows(n, width):
    return tail_rows(12 + -(-n // width))


def prep_kernel(place_ref, size_ref, f_ref, p_ref, up1_ref, up2_ref, *rest):
    vec_refs, out_ref = rest[:-1], rest[-1]
    n, width = f_ref.shape
    x = (f_ref[...].astype(F32) + p_ref[...].astype(F32)) * size_mask(size_ref[0], width)
    middle = (jnp.sum(x, axis=1, keepdims=True) * (1.0 / width)).astype(BF16).astype(F32)
    lane = lax.broadcasted_iota(jnp.int32, (n, width), 1)
    line = mm(jnp.ones((8, width), F32), jnp.where(lane == 0, middle, 0.0), 1, 1)[0:1]
    count = -(-n // width)
    if count * width > n:
        line = jnp.concatenate([line, jnp.zeros((1, count * width - n), F32)], axis=1)
    rows = []
    for ref in vec_refs:
        rows += pieces_of(ref[...], 2)
    rows += flat_rows(line, width)
    part = (out_ref.shape[1] - n - tail_rows(len(rows))) // 2
    start = pl.multiple_of(place_ref[0] * part, part)
    up = [r[pl.ds(start, part), :].astype(BF16) for r in (up1_ref, up2_ref)]
    value = jnp.concatenate([(x - middle).astype(BF16), pack(rows, width)] + up, axis=0)
    put_all(out_ref, value)


def lead_of(x_ref, n):
    width = x_ref.shape[2]
    return [x_ref[j, n : n + lead_rows(n, width), :].astype(F32) for j in range(x_ref.shape[0])]


def restore_x(x_ref, lead, n):
    blocks, _, width = x_ref.shape
    count = -(-n // width)
    lines = [
        jnp.concatenate([p[12 + k : 13 + k] for k in range(count)], axis=1)[:, :n] for p in lead
    ]
    lines = jnp.concatenate(lines, axis=0)
    shape2 = (blocks, blocks * width)
    col = lax.broadcasted_iota(jnp.int32, shape2, 1).astype(F32)
    home = lax.broadcasted_iota(jnp.int32, shape2, 0).astype(F32)
    here = jnp.floor((col + 0.5) * (1.0 / width)) == home
    spread = mm(lines, jnp.where(here, 1.0, 0.0).astype(F32), 0, 0)
    return wide_rows(x_ref, 0, n).astype(F32) + spread


def unpack_up_kernel(images, slot_ref, *refs):
    parts, (up1_ref, up2_ref, buf_ref, sems) = refs[:images], refs[images:]
    fetch(slot_ref, parts, buf_ref, sems, whole_ref)
    arrive(parts, buf_ref, sems, whole_ref)
    q = buf_ref.shape[2] // 2
    for s in range(images):
        both = jnp.concatenate([buf_ref[s, j] for j in range(buf_ref.shape[1])], axis=1)
        up1_ref[s * q : (s + 1) * q, :] = both[:q]
        up2_ref[s * q : (s + 1) * q, :] = both[q:]


def unpack_up(slot, parts, se, channels):
    images = len(parts)
    return pl.pallas_call(
        partial(unpack_up_kernel, images),
        out_shape=[shape((se, channels), BF16), shape((se, channels), BF16)],
        in_specs=[pl.BlockSpec(memory_space=pltpu.SMEM)] + any_specs(images),
        out_specs=[pl.BlockSpec(memory_space=pltpu.VMEM)] * 2,
        scratch_shapes=[
            pltpu.VMEM((images,) + parts[0].shape, BF16), pltpu.SemaphoreType.DMA((images,))
        ],
        cost_estimate=cost(1e6, 2e6),
        name="unpack_up",
    )(slot, *parts)


def norm_rows(x, gain, bias):
    scale = 1.0 / x.shape[1]
    center = jnp.sum(x, axis=1, keepdims=True) * scale
    d = x - center
    inv = lax.rsqrt(jnp.sum(d * d, axis=1, keepdims=True) * scale + EPS)
    normed = d * inv
    return normed, inv, normed * gain + bias


def front_kernel(
    size_ref, x_ref, w_ref, cb_ref, pp_ref, down_ref, vec_ref, h_ref, pay_ref, a_ref, b_ref, sq_ref
):
    out = w_ref.shape[2]
    blocks = x_ref.shape[0]
    n = SIDE * SIDE
    packed = lead_of(x_ref, n)
    x = restore_x(x_ref, packed, n)
    a_ref[...] = split_mm(pp_ref[...], x, 1, 0)
    for k in range(6):
        vec_ref[k : k + 1] = jnp.concatenate(
            [p[2 * k : 2 * k + 1] + p[2 * k + 1 : 2 * k + 2] for p in packed], axis=1
        )
    vec_ref[6:8] = jnp.zeros((2, vec_ref.shape[1]), F32)
    _, _, pre = norm_rows(x, vec_ref[0:1], vec_ref[1:2])
    mask = size_mask(size_ref[0], out)
    h = (silu(pre) * jnp.concatenate([mask] * blocks, axis=1)).astype(BF16)
    h_ref[...] = h
    y = mm(h, wide(w_ref), 1, 0)
    conv = (tap_sum(y, SIDE, out) + cb_ref[...]) * mask
    pooled = split_mm(pp_ref[...], conv, 1, 0)
    b_ref[...] = pooled
    sq = jnp.sum(conv, axis=0, keepdims=True) * per_side(size_ref[0], out)
    sq_ref[...] = sq
    tail = pack32(flat_rows(small_mm(sq, down_ref[...], 0), out), out)
    put_all(pay_ref, jnp.concatenate([pooled, tail], axis=0))


def early_slope_kernel(size_ref, x_ref, vec_ref, n_ref, i_ref, d_ref):
    blocks, _, width = x_ref.shape
    x = restore_x(x_ref, lead_of(x_ref, SIDE * SIDE), SIDE * SIDE)
    normed, inv, pre = norm_rows(x, vec_ref[0:1], vec_ref[1:2])
    n_ref[...] = normed
    i_ref[...] = jnp.broadcast_to(inv, i_ref.shape)
    mask = size_mask(size_ref[0], width)
    d_ref[...] = silu_grad(pre) * jnp.concatenate([mask] * blocks, axis=1)


def late_kernel(
    ball_ref, a_ref, up_all_ref, db_ref, vec_ref, up_ref, ub_ref, w_ref, cb_ref, down_ref,
    h_ref, pool_ref, pay_ref, conv_ref, sq_ref, rpre_ref, e_ref, eall_ref,
):
    out = w_ref.shape[2]
    n = GRID * GRID
    rpre = plain_join(block_sum(ball_ref, n, ball_ref.shape[1]), db_ref.shape[1]) + db_ref[...]
    rpre_ref[...] = rpre
    red = silu(rpre)
    e_all = sigmoid(two_mm(red, up_all_ref[...], 0) + vec_ref[4:5])
    eall_ref[...] = e_all
    e_ref[...] = sigmoid(small_mm(red, up_ref[...], 0) + ub_ref[...])
    pooled = a_ref[...] + wide_rows(ball_ref, 0, n) * e_all
    pool_ref[...] = pooled
    _, _, pre = norm_rows(pooled, vec_ref[2:3], vec_ref[3:4])
    h = silu(pre).astype(BF16)
    h_ref[...] = h
    y = mm(h, wide(w_ref), 1, 0)
    conv = tap_sum(y, GRID, out) + cb_ref[...]
    conv_ref[...] = conv
    sq = jnp.sum(conv, axis=0, keepdims=True) * (1.0 / n)
    sq_ref[...] = sq
    tail = pack32(flat_rows(small_mm(sq, down_ref[...], 0), out), out)
    put_all(pay_ref, jnp.concatenate([conv, tail], axis=0))


def late_slope_kernel(pool_ref, vec_ref, n_ref, i_ref, d_ref):
    normed, inv, pre = norm_rows(pool_ref[...], vec_ref[2:3], vec_ref[3:4])
    n_ref[...] = normed
    i_ref[...] = jnp.broadcast_to(inv, i_ref.shape)
    d_ref[...] = silu_grad(pre)


def put_blocks(ref, values, tails):
    step = ref.shape[2]
    for j in range(ref.shape[0]):
        tail = tails if not isinstance(tails, list) else tails[j]
        block = values[:, j * step : (j + 1) * step].astype(BF16)
        ref[j] = jnp.concatenate([block, tail], axis=0)


def readout_kernel(
    call_ref, pool_ref, up_all_ref, db_ref, vec_ref, up_ref, ub_ref, w_ref, b_ref, *rest
):
    gh_refs = rest[:-7]
    t_ref, act_ref, gp_ref, pay_ref, rpre_ref, e_ref, spare_ref = rest[-7:]
    n = GRID * GRID
    width = pay_ref.shape[2]
    rpre = plain_join(block_sum(call_ref, n, call_ref.shape[1]), db_ref.shape[1]) + db_ref[...]
    rpre_ref[...] = rpre
    red = silu(rpre)
    e_all = sigmoid(two_mm(red, up_all_ref[...], 0) + vec_ref[5:6])
    spare_ref[...] = e_all
    e_ref[...] = sigmoid(small_mm(red, up_ref[...], 0) + ub_ref[...])
    conv = wide_rows(call_ref, 0, n)
    tok = (pool_ref[...] + conv * e_all).astype(BF16)
    t_ref[...] = tok
    pre = mm(tok, w_ref[...], 1, 0) + b_ref[...]
    phi = 0.5 * (1.0 + lax.erf(pre * 0.7071067811865476))
    act_ref[...] = (pre * phi).astype(BF16)
    dens = 0.3989422804014327 * jnp.exp(-0.5 * pre * pre)
    gh = gh_refs[0][...].astype(F32)
    for one in gh_refs[1:]:
        gh = gh + one[...].astype(F32)
    gp = (gh * (phi + pre * dens)).astype(BF16)
    gp_ref[...] = gp
    gt = mm(gp, w_ref[...], 1, 1)
    gl = jnp.sum(gt * conv, axis=0, keepdims=True) * e_all * (1.0 - e_all)
    put_blocks(pay_ref, gt, pack(chop(two_mm(gl, up_all_ref[...], 1), width), width))


def act_grad_kernel(order_ref, g_ref, w_ref, out_ref):
    out_ref[0] = mm(g_ref[...], w_ref[...], 1, 1).astype(BF16)


def logits_kernel(blocks_ref, a0_ref, a1_ref, w_ref, b_ref, out_ref, acc_ref):
    j = pl.program_id(0)
    half = pl.num_programs(0) // 2

    @pl.when(j == 0)
    def _():
        acc_ref[...] = jnp.zeros_like(acc_ref)

    @pl.when(j < half)
    def _():
        acc_ref[...] += mm(a0_ref[0], w_ref[...], 1, 0)

    @pl.when(j >= half)
    def _():
        acc_ref[...] += mm(a1_ref[0], w_ref[...], 1, 0)

    @pl.when(j == pl.num_programs(0) - 1)
    def _():
        out_ref[...] = (acc_ref[...] + b_ref[...]).astype(BF16)


def squeeze_back(gr, rpre_ref, down_ref, grp_ref):
    grp = gr * silu_grad(rpre_ref[...])
    grp_ref[...] = grp
    return small_mm(grp, down_ref[...], 1)


def norm_back(gh, d_ref, n_ref, i_ref, gain):
    normed = n_ref[...]
    gpre = gh * d_ref[...]
    scale = 1.0 / gh.shape[1]
    g_gain = jnp.sum(gpre * normed, axis=0, keepdims=True)
    g_bias = jnp.sum(gpre, axis=0, keepdims=True)
    gn = gpre * gain
    m1 = jnp.sum(gn, axis=1, keepdims=True) * scale
    m2 = jnp.sum(gn * normed, axis=1, keepdims=True) * scale
    return (gn - m1 - normed * m2) * i_ref[:, 0:1], g_gain, g_bias


def gain_tails(extra, g_gain, g_bias, width, blocks):
    tails = []
    for j in range(blocks):
        rows = list(extra)
        for v in (g_gain, g_bias):
            rows += pieces_of(v[:, j * width : (j + 1) * width], 3)
        tails.append(pack(rows, width))
    return tails


def late_back_kernel(
    me_ref, gt_ref, conv_ref, e_ref, rpre_ref, down_ref, w_ref, n_ref, i_ref, d_ref, vec_ref,
    ball_ref, eall_ref, up_all_ref, gc_ref, grp_ref, gl_ref, pay_ref,
):
    out = w_ref.shape[2]
    blocks = pay_ref.shape[0]
    n = GRID * GRID
    se = rpre_ref.shape[1]
    g = block_sum(gt_ref, 0, n)
    e = e_ref[...]
    gl_ref[...] = jnp.sum(g * conv_ref[...], axis=0, keepdims=True) * e * (1.0 - e)
    gr = join(block_sum(gt_ref, n, gt_ref.shape[1]), 0, se)
    gs = squeeze_back(gr, rpre_ref, down_ref, grp_ref)
    gc = (g * e + gs * (1.0 / n)).astype(BF16)
    gc_ref[...] = gc
    gh = mm(tap_spread(gc.astype(F32), GRID, out), wide(w_ref), 1, 1)
    part, g_gain, g_bias = norm_back(gh, d_ref, n_ref, i_ref, vec_ref[2:3])
    own = [g * jnp.where(me_ref[0] == j, 1.0, 0.0).astype(F32) for j in range(blocks)]
    part = part + jnp.concatenate(own, axis=1)
    e_all = eall_ref[...]
    pooled = wide_rows(ball_ref, 0, n)
    gl1 = jnp.sum(part * pooled, axis=0, keepdims=True) * e_all * (1.0 - e_all)
    extra = chop(two_mm(gl1, up_all_ref[...], 1), out)
    put_blocks(pay_ref, part, gain_tails(extra, g_gain, g_bias, out, blocks))


def early_back_kernel(
    size_ref, p2_ref, b_ref, e_ref, rpre_ref, down_ref, pp_ref, w_ref, n_ref, i_ref, d_ref, vec_ref,
    gae_ref, gc_ref, grp_ref, gl_ref, gg_ref, pay_ref,
):
    out = w_ref.shape[2]
    blocks = pay_ref.shape[0]
    n2 = GRID * GRID
    se = rpre_ref.shape[1]
    g = block_sum(p2_ref, 0, n2)
    tail = block_sum(p2_ref, n2, p2_ref.shape[1])
    e = e_ref[...]
    gl_ref[...] = jnp.sum(g * b_ref[...], axis=0, keepdims=True) * e * (1.0 - e)
    used = 3 * (se // out)
    gg_ref[0:1] = join(tail, used, out)
    gg_ref[1:2] = join(tail, used + 3, out)
    gs = squeeze_back(join(tail, 0, se), rpre_ref, down_ref, grp_ref) * per_side(size_ref[0], out)
    gae = split_mm(pp_ref[...], g, 0, 0)
    gae_ref[...] = gae
    gc = ((gae * e + gs) * size_mask(size_ref[0], out)).astype(BF16)
    gc_ref[...] = gc
    gh = mm(tap_spread(gc.astype(F32), SIDE, out), wide(w_ref), 1, 1)
    part, g_gain, g_bias = norm_back(gh, d_ref, n_ref, i_ref, vec_ref[0:1])
    put_blocks(pay_ref, part, gain_tails([], g_gain, g_bias, out, blocks))


def final_kernel(size_ref, p1_ref, gae_ref, fg_ref, low_ref):
    n, width = gae_ref.shape
    out = (gae_ref[...] + block_sum(p1_ref, 0, n)) * size_mask(size_ref[0], width)
    fg_ref[...] = out
    tail = block_sum(p1_ref, n, p1_ref.shape[1])
    rows = []
    for k in range(2):
        rows += pieces_of(join(tail, 3 * k, width), 3)
    low_ref[...] = jnp.concatenate([out.astype(BF16), pack(rows, width)], axis=0)


def fetch(slot_ref, refs, dst_ref, sems, pick):
    for s in range(len(refs)):
        for q, ref in enumerate(refs):

            @pl.when(slot_ref[s] == q)
            def _():
                pltpu.make_async_copy(pick(ref), dst_ref.at[s], sems.at[s]).start()


def arrive(refs, dst_ref, sems, pick):
    for s in range(len(refs)):
        pltpu.make_async_copy(pick(refs[0]), dst_ref.at[s], sems.at[s]).wait()


def any_specs(count):
    return [pl.BlockSpec(memory_space=pl.ANY)] * count


def whole_ref(ref):
    return ref


def position_kernel(images, slot_ref, *refs):
    lows, (pos_ref, gg_ref, buf_ref, sems) = refs[:images], refs[images:]
    fetch(slot_ref, lows, buf_ref, sems, whole_ref)
    arrive(lows, buf_ref, sems, whole_ref)
    n = pos_ref.shape[0]
    acc = buf_ref[0].astype(F32)
    for s in range(1, images):
        acc = acc + buf_ref[s].astype(F32)
    pos_ref[...] = acc[:n]
    for k in range(2):
        gg_ref[k : k + 1] = join(acc[n:], 3 * k, acc.shape[1])


def position_sum(slot, lows):
    images = len(lows)
    tall, width = lows[0].shape
    n = SIDE * SIDE
    return pl.pallas_call(
        partial(position_kernel, images),
        out_shape=[shape((n, width)), shape((2, width))],
        in_specs=[pl.BlockSpec(memory_space=pltpu.SMEM)] + any_specs(images),
        out_specs=[pl.BlockSpec(memory_space=pltpu.VMEM)] * 2,
        scratch_shapes=[
            pltpu.VMEM((images, tall, width), BF16), pltpu.SemaphoreType.DMA((images,))
        ],
        cost_estimate=cost(1e6, images * tall * width * 2),
        name="position",
    )(slot, *lows)


def parcel_kernel(g1_ref, g2_ref, *refs):
    vecs, out_ref = refs[:-1], refs[-1]
    width = out_ref.shape[1]
    rows = []
    for ref in vecs[:2]:
        rows += chop(silu(ref[...]), width)
    for ref in vecs[2:8]:
        rows += chop(ref[...], width)
    rows += chop(vecs[8][0:1], width) + chop(vecs[8][1:2], width)
    out_ref[...] = jnp.concatenate([g1_ref[...], g2_ref[...], pack(rows, width)], axis=0)


def small_kernel(images, se, slot_ref, *refs):
    parcels = refs[:images]
    d1_ref, u1_ref, d2_ref, u2_ref, flat_ref, wide_ref, buf_ref, sems = refs[images:]
    first = SIDE * SIDE + GRID * GRID
    count = buf_ref.shape[1]

    def pick(ref):
        return ref.at[pl.ds(first, count), :]

    fetch(slot_ref, parcels, buf_ref, sems, pick)
    arrive(parcels, buf_ref, sems, pick)
    width = buf_ref.shape[2]
    lengths = [se] * 4 + [width] * 6
    tables = []
    at = 0
    tails = [buf_ref[s].astype(F32) for s in range(images)]
    for length in lengths:
        index = lax.broadcasted_iota(jnp.int32, (8, length), 0)
        table = jnp.zeros((8, length), F32)
        for s in range(images):
            table = jnp.where(index == s, join(tails[s], at, length), table)
        tables.append(table)
        at += 3 * (length // width)
    u1_ref[...] = mm(tables[0], tables[4], 0, 0, HI)
    u2_ref[...] = mm(tables[1], tables[5], 0, 0, HI)
    d1_ref[...] = mm(tables[6], tables[2], 0, 0, HI)
    d2_ref[...] = mm(tables[7], tables[3], 0, 0, HI)
    for k, table in enumerate(tables[2:4]):
        flat_ref[k : k + 1] = jnp.sum(table, axis=0, keepdims=True)
    for k, t in enumerate((4, 5, 8, 9)):
        wide_ref[k : k + 1] = jnp.sum(tables[t], axis=0, keepdims=True)


def small_grads(slot, parcels, se):
    images = len(parcels)
    tall, width = parcels[0].shape
    outs = [(width, se), (se, width), (width, se), (se, width), (2, se), (4, width)]
    return pl.pallas_call(
        partial(small_kernel, images, se),
        out_shape=[shape(o) for o in outs],
        in_specs=[pl.BlockSpec(memory_space=pltpu.SMEM)] + any_specs(images),
        out_specs=[pl.BlockSpec(memory_space=pltpu.VMEM)] * 6,
        scratch_shapes=[
            pltpu.VMEM((images, tall - SIDE * SIDE - GRID * GRID, width), BF16),
            pltpu.SemaphoreType.DMA((images,)),
        ],
        cost_estimate=cost(1e6, 1e6),
        name="small_grads",
    )(slot, *parcels)


def spread_all(images, side, g_ref, spread_ref, gb_ref):
    n = side * side
    total = None
    for s in range(images):
        g = g_ref[s].astype(F32)
        one = jnp.sum(g, axis=0, keepdims=True)
        total = one if total is None else total + one
        spread_ref[s * n : (s + 1) * n, :] = tap_spread(g, side, g.shape[1])
    gb_ref[...] = total


def early_weight_kernel(images, slot_ref, *refs):
    hids, parcels = refs[:images], refs[images : 2 * images]
    out_ref, gb_ref, h_ref, g_ref, spread_ref, sems, sems2 = refs[2 * images :]
    n = SIDE * SIDE
    out = g_ref.shape[2]
    step = pl.program_id(0)
    width = out_ref.shape[1]

    def pick(ref):
        return ref.at[pl.ds(0, n), :]

    @pl.when(step == 0)
    def _():
        fetch(slot_ref, parcels, g_ref, sems2, pick)
        fetch(slot_ref, hids, h_ref, sems, whole_ref)
        arrive(parcels, g_ref, sems2, pick)
        spread_all(images, SIDE, g_ref, spread_ref, gb_ref)
        arrive(hids, h_ref, sems, whole_ref)

    lanes = pl.ds(pl.multiple_of(step * width, width), width)
    h = jnp.concatenate([h_ref[s, :, lanes] for s in range(images)], axis=0)
    res = mm(h, spread_ref[...], 0, 0)
    for t in range(9):
        out_ref[t] = res[:, t * out : (t + 1) * out]


def early_weights(slot, hids, parcels, steps):
    images = len(hids)
    n, channels = hids[0].shape
    out = parcels[0].shape[1]
    rows = channels // steps
    return pl.pallas_call(
        partial(early_weight_kernel, images),
        out_shape=[shape((9, channels, out)), shape((1, out))],
        grid_spec=pltpu.PrefetchScalarGridSpec(
            num_scalar_prefetch=1,
            grid=(steps,),
            in_specs=any_specs(2 * images),
            out_specs=[
                pl.BlockSpec((9, rows, out), lambda k, s: (0, k, 0)),
                pl.BlockSpec((1, out), lambda k, s: (0, 0)),
            ],
            scratch_shapes=[
                pltpu.VMEM((images, n, channels), BF16),
                pltpu.VMEM((images, n, out), BF16),
                pltpu.VMEM((images * n, 9 * out), BF16),
                pltpu.SemaphoreType.DMA((images,)),
                pltpu.SemaphoreType.DMA((images,)),
            ],
        ),
        cost_estimate=cost(
            2 * images * n * 9 * out * channels, images * n * channels * 2 + 36 * channels * out
        ),
        name="early_weights",
    )(slot, *hids, *parcels)


def late_weight_kernel(images, channels, cols, slot_ref, *refs):
    cats, parcels = refs[:images], refs[images : 2 * images]
    w_ref, gb_ref, in_ref, ib_ref, c_ref, g_ref, spread_ref, sems, sems2 = refs[2 * images :]
    n = GRID * GRID
    out = g_ref.shape[2]
    step = pl.program_id(0)
    width = w_ref.shape[1]

    def pick_cat(ref):
        return ref.at[:, pl.ds(0, c_ref.shape[2])]

    def pick(ref):
        return ref.at[pl.ds(SIDE * SIDE, n), :]

    @pl.when(step == 0)
    def _():
        fetch(slot_ref, parcels, g_ref, sems2, pick)
        fetch(slot_ref, cats, c_ref, sems, pick_cat)
        arrive(parcels, g_ref, sems2, pick)
        spread_all(images, GRID, g_ref, spread_ref, gb_ref)
        arrive(cats, c_ref, sems, pick_cat)

    gp = jnp.concatenate([c_ref[s, :, 2 * channels :] for s in range(images)], axis=0)

    @pl.when(step == 0)
    def _():
        ib_ref[...] = jnp.sum(gp.astype(F32), axis=0, keepdims=True)

    lanes = pl.ds(pl.multiple_of(step * width, width), width)
    tok = jnp.concatenate([c_ref[s, :, lanes] for s in range(images)], axis=0)
    in_ref[...] = mm(tok, gp, 0, 0)
    lanes = pl.ds(pl.multiple_of(step * width + channels, width), width)
    h = jnp.concatenate([c_ref[s, :, lanes] for s in range(images)], axis=0)
    res = mm(h, spread_ref[...], 0, 0)
    for t in range(9):
        w_ref[t] = res[:, t * out : (t + 1) * out]


def late_weights(slot, cats, parcels, channels, cols, steps):
    images = len(cats)
    n = cats[0].shape[0]
    out = parcels[0].shape[1]
    rows = channels // steps
    return pl.pallas_call(
        partial(late_weight_kernel, images, channels, cols),
        out_shape=[
            shape((9, channels, out)), shape((1, out)), shape((channels, cols)), shape((1, cols))
        ],
        grid_spec=pltpu.PrefetchScalarGridSpec(
            num_scalar_prefetch=1,
            grid=(steps,),
            in_specs=any_specs(2 * images),
            out_specs=[
                pl.BlockSpec((9, rows, out), lambda k, s: (0, k, 0)),
                pl.BlockSpec((1, out), lambda k, s: (0, 0)),
                pl.BlockSpec((rows, cols), lambda k, s: (k, 0)),
                pl.BlockSpec((1, cols), lambda k, s: (0, 0)),
            ],
            scratch_shapes=[
                pltpu.VMEM((images, n, 2 * channels + cols), BF16),
                pltpu.VMEM((images, n, out), BF16),
                pltpu.VMEM((images * n, 9 * out), BF16),
                pltpu.SemaphoreType.DMA((images,)),
                pltpu.SemaphoreType.DMA((images,)),
            ],
        ),
        cost_estimate=cost(2 * images * n * (9 * out + cols) * channels, 12e6),
        name="late_weights",
    )(slot, *cats, *parcels)


def act_weight_kernel(images, offset, slot_ref, blocks_ref, *refs):
    act0, act1, cats = (refs[k * images : (k + 1) * images] for k in range(3))
    out_ref, gb_ref, a_ref, g_ref, sems0, sems1, sems2 = refs[3 * images :]
    j = pl.program_id(0)
    half = pl.num_programs(0) // 2

    def pick(ref):
        return ref.at[:, pl.ds(offset, g_ref.shape[2])]

    @pl.when(j == 0)
    def _():
        fetch(slot_ref, cats, g_ref, sems2, pick)
        fetch(slot_ref, act0, a_ref.at[0], sems0, whole_ref)
        fetch(slot_ref, act1, a_ref.at[1], sems1, whole_ref)
        arrive(cats, g_ref, sems2, pick)
        arrive(act0, a_ref.at[0], sems0, whole_ref)

    @pl.when(j == half)
    def _():
        arrive(act1, a_ref.at[1], sems1, whole_ref)

    g = jnp.concatenate([g_ref[s] for s in range(images)], axis=0)

    @pl.when(j == 0)
    def _():
        gb_ref[...] = jnp.sum(g.astype(F32), axis=0, keepdims=True)

    side = j // half
    k = j % half
    a = jnp.concatenate([a_ref[side, s, k] for s in range(images)], axis=0)
    out_ref[...] = mm(a, g, 0, 0)


def act_weights(slot, blocks, act0, act1, cats, offset, cols):
    images = len(act0)
    half, rows, width = act0[0].shape
    total = 2 * half
    return pl.pallas_call(
        partial(act_weight_kernel, images, offset),
        out_shape=[shape((total * width, cols)), shape((1, cols))],
        grid_spec=pltpu.PrefetchScalarGridSpec(
            num_scalar_prefetch=2,
            grid=(total,),
            in_specs=any_specs(3 * images),
            out_specs=[
                pl.BlockSpec((width, cols), lambda k, s, b: (b[k], 0)),
                pl.BlockSpec((1, cols), lambda k, s, b: (0, 0)),
            ],
            scratch_shapes=[
                pltpu.VMEM((2, images, half, rows, width), BF16),
                pltpu.VMEM((images, rows, cols), BF16),
            ]
            + [pltpu.SemaphoreType.DMA((images,))] * 3,
        ),
        cost_estimate=cost(
            2 * images * rows * total * width * cols, images * total * rows * width * 2 + total * width * cols * 4
        ),
        name="act_weights",
    )(slot, blocks, *act0, *act1, *cats)


def swap(v):
    return lax.all_to_all(v, "mp", 0, 0)


def permute(v, axis, fn):
    n = lax.axis_size(axis)
    return lax.ppermute(v, axis, [(i, fn(i) % n) for i in range(n)])


def dp_gather(v, relay=True):
    n = lax.axis_size("dp")
    slots = [v, permute(v, "dp", lambda i: i ^ 1)]
    for k in range(1, n // 2):
        far = permute(v, "dp", lambda i: i + 2 * k)
        slots.append(far)
        if relay:
            slots.append(permute(far, "dp", lambda i: i ^ 1))
        else:
            slots.append(permute(v, "dp", lambda i: ((i + 2 * k) % n) ^ 1))
    return slots


def after(v, *deps):
    return lax.optimization_barrier((v,) + deps)[0]


def dp_slots():
    n = lax.axis_size("dp")
    me = lax.axis_index("dp")
    s = jnp.arange(n)
    hops = (me // 2 - s // 2) % (n // 2)
    return (2 * hops + ((s ^ me) & 1)).astype(jnp.int32)


def row(v):
    return v.reshape(1, -1)


def per_device(
    features,
    position,
    image_sizes,
    gain_early,
    bias_early,
    conv_early,
    conv_bias_early,
    down_early,
    down_bias_early,
    up_early,
    up_bias_early,
    gain_late,
    bias_late,
    conv_late,
    conv_bias_late,
    down_late,
    down_bias_late,
    up_late,
    up_bias_late,
    readout_in,
    readout_in_bias,
    readout_out,
    readout_out_bias,
    out_grad,
):
    mp = lax.axis_size("mp")
    dp = lax.axis_size("dp")
    width = features.shape[0]
    channels = width * mp
    n = SIDE * SIDE
    n2 = GRID * GRID
    se = down_early.shape[1]
    cols = readout_in.shape[1]
    out_cols = readout_out.shape[1]
    half = mp // 2
    slot = dp_slots()
    me = lax.axis_index("mp")
    place = lax.axis_index("dp").reshape(1).astype(jnp.int32)
    mine = me.reshape(1).astype(jnp.int32)
    step = jnp.arange(half)
    sides = (me % 2) ^ jnp.arange(2)[:, None]
    send_order = (((me // 2 + step) % half)[None] * 2 + sides).reshape(-1).astype(jnp.int32)
    got_order = (((me // 2 - step) % half)[None] * 2 + sides).reshape(-1).astype(jnp.int32)

    feats = jnp.transpose(features.reshape(width, n))
    posn = jnp.transpose(position)
    w_early = jnp.transpose(conv_early, (1, 0, 2))
    w_late = jnp.transpose(conv_late, (1, 0, 2))
    pool = jnp.where(
        image_sizes[0] == SIDE, pool_matrix(SIDE, SIDE, GRID), pool_matrix(SMALL, SIDE, GRID)
    )
    pp = (pool[:, None, :, None] * pool[None, :, None, :]).reshape(n2, n).astype(BF16)
    vecs = (gain_early, bias_early, gain_late, bias_late, up_bias_early, up_bias_late)
    part = se // dp
    up_at = n + lead_rows(n, width)
    tall = up_at + 2 * part
    (pay,) = call(
        prep_kernel, (shape((mp, tall, width), BF16),), place, image_sizes, feats, posn,
        up_early, up_late, *[row(v) for v in vecs], smem=(0, 1), name="prep",
    )
    x_all = swap(pay)

    gact = pl.pallas_call(
        act_grad_kernel,
        out_shape=shape((mp, n2, cols), BF16),
        grid_spec=pltpu.PrefetchScalarGridSpec(
            num_scalar_prefetch=1,
            grid=(mp,),
            in_specs=[
                pl.BlockSpec((n2, out_cols), lambda j, o: (0, 0)),
                pl.BlockSpec((cols, out_cols), lambda j, o: (o[j], 0)),
            ],
            out_specs=pl.BlockSpec((1, n2, cols), lambda j, o: (j, 0, 0)),
        ),
        cost_estimate=cost(2 * n2 * out_cols * cols * mp, cols * mp * out_cols * 2),
        name="act_grad",
    )(send_order, out_grad, readout_out)
    theirs = permute(gact[half:], "mp", lambda i: i ^ 1)
    gact = (gact[:half].astype(F32) + theirs.astype(F32)).astype(BF16)
    x_all = after(x_all, gact)
    gact = [gact[0]] + [permute(gact[k], "mp", lambda i: i + 2 * k) for k in range(1, half)]

    up1_all, up2_all = unpack_up(slot, dp_gather(x_all[:, up_at:]), se, channels)
    tail0 = -(-(se // width) // 8) * 8
    tail1 = tail_rows(3 * (se // width))
    tail2 = tail_rows(3 * (se // width) + 6)
    vec_all, hid, pay, pool_a, pool_b, sq1 = call(
        front_kernel,
        (
            shape((8, channels)), shape((n, channels), BF16), shape((mp, n2 + tail0, width)),
            shape((n2, channels)), shape((n2, width)), shape((1, width)),
        ),
        image_sizes, x_all, w_early, row(conv_bias_early), pp, down_early,
        smem=(0,), flops=2 * n * channels * 9 * width, name="front",
    )
    b_all = swap(pay)
    normed1, inv1, slope1 = call(
        early_slope_kernel,
        (shape((n, channels)), shape((n, 128)), shape((n, channels))),
        image_sizes, x_all, vec_all, smem=(0,), name="early_slope",
    )
    hids = dp_gather(hid)
    b_all = after(b_all, slope1, *gact[1:])
    hid2, pooled, pay, conv2, sq2, rpre1, e1, e1_all = call(
        late_kernel,
        (
            shape((n2, channels), BF16), shape((n2, channels)), shape((mp, n2 + tail0, width)),
            shape((n2, width)), shape((1, width)), shape((1, se)), shape((1, width)),
            shape((1, channels)),
        ),
        b_all, pool_a, up1_all, row(down_bias_early), vec_all, up_early, row(up_bias_early),
        w_late, row(conv_bias_late), down_late,
        flops=2 * n2 * channels * 9 * width, name="late",
    )
    c_all = swap(pay)
    normed2, inv2, slope2 = call(
        late_slope_kernel,
        (shape((n2, channels)), shape((n2, 128)), shape((n2, channels))),
        pooled, vec_all, name="late_slope",
    )
    c_all = after(c_all, slope2)
    tok, act, gpre, pay, rpre2, e2, _ = call(
        readout_kernel,
        (
            shape((n2, channels), BF16), shape((n2, cols), BF16), shape((n2, cols), BF16),
            shape((mp, n2 + tail1, width), BF16), shape((1, se)), shape((1, width)),
            shape((1, channels)),
        ),
        c_all, pooled, up2_all, row(down_bias_late), vec_all, up_late, row(up_bias_late),
        readout_in, row(readout_in_bias), *gact,
        flops=4 * n2 * channels * cols, name="readout",
    )
    gtok = swap(pay)
    cat = jnp.concatenate([tok, hid2, gpre, out_grad], axis=1)
    cats = dp_gather(cat)
    gtok = after(gtok, cat, *hids[1:3])
    gconv2, grp2, gl2, pay = call(
        late_back_kernel,
        (
            shape((n2, width), BF16), shape((1, se)), shape((1, width)),
            shape((mp, n2 + tail2, width), BF16),
        ),
        mine, gtok, conv2, e2, rpre2, down_late, w_late, normed2, inv2, slope2, vec_all,
        b_all, e1_all, up1_all,
        smem=(0,), flops=2 * n2 * channels * 9 * width, name="late_back",
    )
    acts = [permute(act, "mp", lambda i: i + 2 * k) for k in range(1, half)]
    act0 = jnp.stack([act] + [after(one, grp2) for one in acts])
    act1 = permute(act0, "mp", lambda i: i ^ 1)
    part2 = after(swap(pay), *hids[3:], *cats[1:3])
    gae, gconv1, grp1, gl1, gg2, pay = call(
        early_back_kernel,
        (
            shape((n, width)), shape((n, width), BF16), shape((1, se)), shape((1, width)),
            shape((2, width)), shape((mp, n + 16, width), BF16),
        ),
        image_sizes, part2, pool_b, e1, rpre1, down_early, pp, w_early, normed1, inv1, slope1, vec_all,
        smem=(0,), flops=2 * n * channels * 9 * width, name="early_back",
    )
    part1 = swap(after(pay, *acts))
    (parcel,) = call(
        parcel_kernel, (shape((n + n2 + tail_rows(12 * (se // width) + 18), width), BF16),),
        gconv1, gconv2, rpre1, rpre2, grp1, grp2, gl1, gl2, sq1, sq2, gg2, name="parcel",
    )
    parcels = dp_gather(parcel, relay=False)
    grad_w2, grad_cb2, grad_in_w, grad_in_b = late_weights(slot, cats, parcels, channels, cols, 2)
    grad_w1, grad_cb1 = early_weights(slot, hids, parcels, 2)
    act1 = after(act1, grad_cb1)
    tokens_out = pl.pallas_call(
        logits_kernel,
        out_shape=shape((n2, out_cols), BF16),
        grid_spec=pltpu.PrefetchScalarGridSpec(
            num_scalar_prefetch=1,
            grid=(mp,),
            in_specs=[
                pl.BlockSpec((1, n2, cols), lambda j, o: (jnp.minimum(j, half - 1), 0, 0)),
                pl.BlockSpec((1, n2, cols), lambda j, o: (jnp.maximum(j - half, 0), 0, 0)),
                pl.BlockSpec((cols, out_cols), lambda j, o: (o[j], 0)),
                pl.BlockSpec((1, out_cols), lambda j, o: (0, 0)),
            ],
            out_specs=pl.BlockSpec((n2, out_cols), lambda j, o: (0, 0)),
            scratch_shapes=[pltpu.VMEM((n2, out_cols), F32)],
        ),
        cost_estimate=cost(2 * n2 * out_cols * cols * mp, cols * mp * out_cols * 2),
        name="logits",
    )(got_order, act0, act1, readout_out, row(readout_out_bias))

    grad_down1, grad_up1, grad_down2, grad_up2, flat, lines = small_grads(slot, parcels, se)
    part1 = after(part1, grad_w1, grad_w2, flat, tokens_out)
    fgrad, low = call(
        final_kernel, (shape((n, width)), shape((n + 16, width), BF16)),
        image_sizes, part1, gae, smem=(0,), name="final",
    )
    pos_grad, gg1 = position_sum(slot, dp_gather(low, relay=False))
    grad_out_w, grad_out_b = act_weights(
        slot, got_order, dp_gather(act0), dp_gather(act1), cats, 2 * channels + cols, out_cols
    )

    return (
        tokens_out,
        jnp.transpose(fgrad).reshape(width, 1, n),
        jnp.transpose(pos_grad),
        gg1[0],
        gg1[1],
        jnp.transpose(grad_w1, (1, 0, 2)),
        grad_cb1[0],
        grad_down1,
        flat[0],
        grad_up1,
        lines[0],
        lines[2],
        lines[3],
        jnp.transpose(grad_w2, (1, 0, 2)),
        grad_cb2[0],
        grad_down2,
        flat[1],
        grad_up2,
        lines[1],
        grad_in_w,
        grad_in_b[0],
        grad_out_w,
        grad_out_b[0],
    )


def solution(mesh):
    by_mp = P("mp")
    block = (by_mp, by_mp, P(None, None, "mp"), by_mp, P("mp", None), P(), P(None, "mp"), by_mp)
    return jax.shard_map(
        per_device,
        mesh=mesh,
        in_specs=(P("mp", "dp", None), P("mp", None), P("dp"))
        + block
        + block
        + (P(None, "mp"), by_mp, P(None, "mp"), by_mp, P("dp", "mp")),
        out_specs=(P("dp", "mp"), P("mp", "dp", None), P("mp", None))
        + block
        + block
        + (P(None, "mp"), by_mp, P(None, "mp"), by_mp),
        check_vma=False,
    )
```
